32 devices in a mesh: parts: 2 (over y), row: 4 (over x, core), col: 4 (over z).
Axes of the slice: x: 2, y: 2, z: 4, core: 2. Of those that a mesh axis runs over, the one named last changes fastest.
Arguments:
- atom_feats: bfloat16 [2048, 128], P(('parts', 'row', 'col')), parts along dimension 0, may hold values from -6 to 6
- atom_bias: bfloat16 [4, 2048, 128], P(None, ('parts', 'row', 'col')), parts along dimension 1, may hold values from -6 to 300
- key_mask: int32 [64, 128], P(('parts', 'row', 'col')), parts along dimension 0, may hold values 0 or 1
- atom_token: int32 [2048], P('parts'), parts along dimension 0, may hold values from 0 to 191, never falling along the last dimension, each value on 1 to 10 neighbouring positions
- token_mask: int32 [384], P('parts'), parts along dimension 0, may hold values 0 or 1
- pair: bfloat16 [384, 192, 128], P(('parts', 'row'), 'col'), parts along dimension 0, may hold values from -6 to 6
- atom_norms: float32 [3, 2, 128], replicated, may hold values from 0.25 to 1.75
- w_atom_qkv: bfloat16 [3, 128, 384], replicated, may hold values from -0.5 to 0.5
- w_atom_gate: bfloat16 [3, 128, 128], replicated, may hold values from -0.5 to 0.5
- w_atom_out: bfloat16 [3, 128, 128], replicated, may hold values from -0.5 to 0.5
- w_atom_up: bfloat16 [3, 128, 512], replicated, may hold values from -0.5 to 0.5
- w_atom_down: bfloat16 [3, 256, 128], replicated, may hold values from -0.375 to 0.375
- w_agg: bfloat16 [128, 768], replicated, may hold values from -0.5 to 0.5
- token_norm: float32 [768], replicated, may hold values from 0.25 to 1.75
- w_token: bfloat16 [4, 768, 384], replicated, may hold values from -0.21875 to 0.21875
- pair_norms: float32 [3, 128], replicated, may hold values from 0.25 to 1.75
- w_pair_up: bfloat16 [2, 128, 1024], replicated, may hold values from -0.5 to 0.5
- w_pair_down: bfloat16 [2, 512, 128], replicated, may hold values from -0.25 to 0.25
- w_bias: float32 [128, 8], replicated, may hold values from -16 to 16
Outputs:
- atom_out: bfloat16 [2048, 128], P(('parts', 'row', 'col')), parts along dimension 0
- token_out: bfloat16 [384, 384], P(('parts', 'row')), parts along dimension 0
The draws below stay inside these ranges and needn't reach their ends.
There are 2 independent parts, one for each index of `parts`. The reference program is written for one: setup_inputs(seed, part) draws one part's arguments, and reference() takes and returns one part's arrays. A program takes and returns all parts, laid end to end along the dimension named above; an argument that names none is the same for every part. Nothing has to cross between parts.
Inputs may be any that keep to these rules, and one draw needn't show every extreme that they name: `atom_token`: token numbers never fall along the atoms; every token has 1 to 10 atoms and some token has exactly 10.
All inputs are finite; a program needn't handle non-finite values. No bound on the sum of `key_mask` on one device may be relied on, other than what follows from the above.
Results may differ from the reference program's by a relative error of at most 0.024.
The reference program's roundings to bfloat16 on the way count: a program that leaves them out, or rounds other values in their place, can miss the bound.
Values may be sent and summed in bfloat16 or wider, within the bound.
No kernel may reach another device: no remote copies, remote signals or barrier semaphores. Data moves between devices by JAX's collectives and lax.ppermute only.
A program may use at most 64 MiB of HBM per device.

```python
import math
import jax
import jax.numpy as jnp
import numpy as np
from jax import lax

C_ATOM = 128
ATOM_HEADS = 4
ATOM_FF = 256
ATOM_BLOCKS = 3
QWIN = 32
KWIN = 128
N_ATOMS = 1024
C_TOKEN = 768
HEADS = 8
HEAD = 48
HD = 384
C_PAIR = 128
PAIR_FF = 512
TRANS = 2
NTOK = 192
MOST_ATOMS = 10
N_ROW = 4


def draw_atom_bias(key, part):
    shape = (ATOM_HEADS, N_ATOMS, KWIN)
    keys = jax.random.split(jax.random.fold_in(key, 11), 1)
    base = jax.random.normal(keys[0], shape, jnp.float32)
    return jnp.clip(base, -6.0, 300.0).astype(jnp.bfloat16)


def draw_w_bias(key, part):
    shape = (C_PAIR, HEADS)
    base = jax.random.normal(jax.random.fold_in(key, 23), shape, jnp.float32)
    return jnp.clip(base * C_PAIR ** (-0.5), -16.0, 16.0)


def set_ends(result, rng, least, largest):
    dims = result.shape
    place = [jax.random.randint(jax.random.fold_in(rng, axis), (), 0, dims[axis]) for axis in range(len(dims))]
    result = result.at[tuple(place)].set(least)
    longest = dims.index(max(dims))
    place[longest] = (place[longest] + 1) % dims[longest]
    return result.at[tuple(place)].set(largest)


def level_of(own_key, shape, pieces, smallest, top_value):
    def one(position, blocks):
        draws = jax.random.uniform(jax.random.fold_in(jax.random.fold_in(own_key, 6), position), (blocks,), jnp.float32, smallest / len(pieces), top_value / len(pieces))
        return jnp.repeat(jnp.exp(draws), shape[position] // blocks).reshape((-1,) + (1,) * (len(shape) - position - 1))

    level = one(*pieces[0])
    for cut in pieces[1:]:
        level = level * one(*cut)
    return level


def split_up(number_of, total, limit, slope):
    portions = [(1 << 20) // math.isqrt(rank ** slope) + 1 for rank in range(2, number_of + 1)]
    spare, given = total - limit - (number_of - 1), [1] * (number_of - 1)
    while spare > 0:
        free = [i for i in range(number_of - 1) if given[i] < limit]
        pool, budget = sum([portions[i] for i in free]), spare
        for i in free:
            addition = min(limit - given[i], max(1, budget * portions[i] // pool), spare)
            given[i] = given[i] + addition
            spare = spare - addition
    return np.array([limit] + given)


def uneven(key, amount, total, reach, lean):
    if amount == 2:
        one = jax.random.randint(key, (), max(1, total - reach), min(reach, total - 1) + 1)
        return jnp.stack([one, total - one])
    tallies = jnp.asarray(split_up(amount, total, reach, lean), jnp.int32)
    pairs = (amount - 1) // 2
    donor, sink = tallies[1:1 + 2 * pairs:2], tallies[2:2 + 2 * pairs:2]
    slack = jnp.minimum(donor - 1, reach - sink)
    shifted = jax.random.randint(jax.random.fold_in(key, 1), (pairs,), 0, 1 << 20) % (slack + 1)
    tallies = tallies.at[1:1 + 2 * pairs:2].set(donor - shifted).at[2:2 + 2 * pairs:2].set(sink + shifted)
    return tallies[jax.random.permutation(jax.random.fold_in(key, 2), amount)]


def gaussian(stream_key, dims, scale, most, shards=(), kind=jnp.bfloat16):
    entries = scale * jax.random.normal(stream_key, dims, jnp.float32)
    if shards:
        entries = entries * level_of(stream_key, dims, shards, -0.22, 0.18)
    return jnp.clip(entries, -most, most).astype(kind)


def setup_inputs(seed: int = 0, part: int = 0) -> dict:
    key_list = jax.random.split(jax.random.key(seed), 20)
    part_keys = jax.random.split(jax.random.fold_in(key_list[19], part), 20)
    atom_feats = gaussian(part_keys[0], (N_ATOMS, C_ATOM), 1.0, 6.0, ((0, 16),))
    atom_bias = draw_atom_bias(jax.random.fold_in(jax.random.fold_in(key_list[19], part), 71), part)
    key_mask = set_ends((jax.random.randint(part_keys[2], (N_ATOMS // QWIN, KWIN), 0, 4) < 3).astype(jnp.int32), jax.random.fold_in(part_keys[2], 1), 0, 1)
    atom_token = jnp.searchsorted(jnp.cumsum(uneven(part_keys[3], NTOK, N_ATOMS, MOST_ATOMS, 2)), jnp.arange(N_ATOMS), side="right").astype(jnp.int32)
    token_mask = set_ends((jax.random.randint(part_keys[4], (NTOK,), 0, 8) < 7).astype(jnp.int32), jax.random.fold_in(part_keys[4], 1), 0, 1)
    pair = gaussian(part_keys[5], (NTOK, NTOK, C_PAIR), 1.0, 6.0, ((0, 4), (1, 4)))
    atom_norms = jnp.clip(1.0 + 0.15 * jax.random.normal(key_list[6], (ATOM_BLOCKS, 2, C_ATOM), jnp.float32), 0.25, 1.75)
    w_atom_qkv = gaussian(key_list[7], (ATOM_BLOCKS, C_ATOM, 3 * C_ATOM), C_ATOM ** -0.5, 0.5)
    w_atom_gate = gaussian(key_list[8], (ATOM_BLOCKS, C_ATOM, C_ATOM), C_ATOM ** -0.5, 0.5)
    w_atom_out = gaussian(key_list[9], (ATOM_BLOCKS, C_ATOM, C_ATOM), C_ATOM ** -0.5, 0.5)
    w_atom_up = gaussian(key_list[10], (ATOM_BLOCKS, C_ATOM, 2 * ATOM_FF), C_ATOM ** -0.5, 0.5)
    w_atom_down = gaussian(key_list[11], (ATOM_BLOCKS, ATOM_FF, C_ATOM), ATOM_FF ** -0.5, 0.375)
    w_agg = gaussian(key_list[12], (C_ATOM, C_TOKEN), C_ATOM ** -0.5, 0.5)
    token_norm = jnp.clip(1.0 + 0.15 * jax.random.normal(key_list[13], (C_TOKEN,), jnp.float32), 0.25, 1.75)
    w_token = gaussian(key_list[14], (4, C_TOKEN, HD), C_TOKEN ** -0.5, 0.21875)
    pair_norms = jnp.clip(1.0 + 0.15 * jax.random.normal(key_list[15], (TRANS + 1, C_PAIR), jnp.float32), 0.25, 1.75)
    w_pair_up = gaussian(key_list[16], (TRANS, C_PAIR, 2 * PAIR_FF), C_PAIR ** -0.5, 0.5)
    w_pair_down = gaussian(key_list[17], (TRANS, PAIR_FF, C_PAIR), PAIR_FF ** -0.5, 0.25)
    w_bias = draw_w_bias(jax.random.fold_in(key_list[19], 71), part)
    return {"atom_feats": atom_feats, "atom_bias": atom_bias, "key_mask": key_mask, "atom_token": atom_token, "token_mask": token_mask, "pair": pair, "atom_norms": atom_norms, "w_atom_qkv": w_atom_qkv, "w_atom_gate": w_atom_gate, "w_atom_out": w_atom_out, "w_atom_up": w_atom_up, "w_atom_down": w_atom_down, "w_agg": w_agg, "token_norm": token_norm, "w_token": w_token, "pair_norms": pair_norms, "w_pair_up": w_pair_up, "w_pair_down": w_pair_down, "w_bias": w_bias}


EPSILON = 1e-05
NEGATIVE = -1e+30

def layer_norm(inputs, gain):
    inputs = inputs.astype(jnp.float32)
    average = lax.optimization_barrier(jnp.mean(inputs, axis=-1, keepdims=True))
    centered = inputs - average
    variance = lax.optimization_barrier(jnp.mean(centered * centered, axis=-1, keepdims=True))
    return centered * lax.rsqrt(variance + EPSILON) * gain

def swiglu(normed, w_up, w_down):
    both_parts = jnp.dot(normed, w_up, preferred_element_type=jnp.float32)
    half_width = both_parts.shape[-1] // 2
    hidden = (jax.nn.silu(both_parts[..., :half_width]) * both_parts[..., half_width:]).astype(jnp.bfloat16)
    return jnp.dot(hidden, w_down, preferred_element_type=jnp.float32)

def atom_block(state, atom_bias, usable, norms, w_qkv, w_gate, w_out, w_up, w_down):
    n_atoms, width = state.shape
    head_size = width // ATOM_HEADS
    margin = (KWIN - QWIN) // 2
    normed = layer_norm(state, norms[0]).astype(jnp.bfloat16)
    qkv = jnp.dot(normed, w_qkv, preferred_element_type=jnp.float32)
    queries = qkv[:, :width].astype(jnp.bfloat16)
    keyvals = qkv[:, width:].astype(jnp.bfloat16)
    padded = jnp.pad(keyvals, ((margin, margin), (0, 0)))
    n_win = n_atoms // QWIN
    window_rows = jnp.arange(n_win, dtype=jnp.int32)[:, None] * QWIN + jnp.arange(KWIN, dtype=jnp.int32)[None, :]
    windows = padded[window_rows]
    key_rows = windows[..., :width].reshape(n_win, KWIN, ATOM_HEADS, head_size).astype(jnp.float32)
    val_rows = windows[..., width:].reshape(n_win, KWIN, ATOM_HEADS, head_size).astype(jnp.float32)
    query_rows = queries.reshape(n_win, QWIN, ATOM_HEADS, head_size).astype(jnp.float32)
    scores = jnp.einsum('wqhd,wkhd->whqk', query_rows, key_rows) / jnp.sqrt(jnp.float32(head_size))
    bias_rows = atom_bias.astype(jnp.float32).reshape(ATOM_HEADS, n_win, QWIN, KWIN).transpose(1, 0, 2, 3)
    scores = scores + bias_rows
    mask_rows = usable[:, None, None, :]
    scores = jnp.where(mask_rows, scores, NEGATIVE)
    row_top = lax.optimization_barrier(jnp.max(scores, axis=-1, keepdims=True))
    weights = jnp.where(mask_rows, jnp.exp(scores - row_top), 0.0)
    totals = lax.optimization_barrier(jnp.sum(weights, axis=-1))
    weighted = jnp.einsum('whqk,wkhd->wqhd', weights.astype(jnp.bfloat16).astype(jnp.float32), val_rows)
    attended = (weighted / totals.transpose(0, 2, 1)[..., None]).reshape(n_atoms, width)
    gate_rows = jax.nn.sigmoid(jnp.dot(normed, w_gate, preferred_element_type=jnp.float32))
    mixed = (gate_rows * attended).astype(jnp.bfloat16)
    state = state + jnp.dot(mixed, w_out, preferred_element_type=jnp.float32)
    normed_two = layer_norm(state, norms[1]).astype(jnp.bfloat16)
    return state + swiglu(normed_two, w_up, w_down)

def reference(atom_feats, atom_bias, key_mask, atom_token, token_mask, pair, atom_norms, w_atom_qkv, w_atom_gate, w_atom_out, w_atom_up, w_atom_down, w_agg, token_norm, w_token, pair_norms, w_pair_up, w_pair_down, w_bias):
    n_atoms = atom_feats.shape[0]
    margin = (KWIN - QWIN) // 2
    n_win = n_atoms // QWIN
    key_slot = jnp.arange(KWIN, dtype=jnp.int32)
    key_index = jnp.arange(n_win, dtype=jnp.int32)[:, None] * QWIN - margin + key_slot[None, :]
    own_window = (key_slot >= margin) & (key_slot < margin + QWIN)
    usable = (key_index >= 0) & (key_index < n_atoms) & (key_mask == 1) | own_window[None, :]
    state = atom_feats.astype(jnp.float32)
    for block_number in range(ATOM_BLOCKS):
        state = atom_block(state, atom_bias, usable, atom_norms[block_number], w_atom_qkv[block_number], w_atom_gate[block_number], w_atom_out[block_number], w_atom_up[block_number], w_atom_down[block_number])
    atom_out = state.astype(jnp.bfloat16)
    feat = jax.nn.relu(jnp.dot(atom_out, w_agg, preferred_element_type=jnp.float32)).astype(jnp.bfloat16)
    sums = jax.ops.segment_sum(feat.astype(jnp.float32), atom_token, num_segments=NTOK)
    counts = jax.ops.segment_sum(jnp.ones((n_atoms,), jnp.float32), atom_token, num_segments=NTOK)
    token_normed = layer_norm(sums / counts[:, None], token_norm).astype(jnp.bfloat16)
    projected = [jnp.dot(token_normed, w_token[which], preferred_element_type=jnp.float32).astype(jnp.bfloat16) for which in range(4)]

    def pair_rows(rows):
        state_z = rows.astype(jnp.float32)
        for which in range(TRANS):
            normed = layer_norm(state_z, pair_norms[which]).astype(jnp.bfloat16)
            state_z = state_z + swiglu(normed, w_pair_up[which], w_pair_down[which])
        final_norm = layer_norm(state_z, pair_norms[TRANS])
        return jnp.einsum('ijc,ch->hij', final_norm, w_bias, precision=lax.Precision.HIGHEST)
    blocks = lax.map(pair_rows, pair.reshape(N_ROW, NTOK // N_ROW, NTOK, pair.shape[2]))
    pair_bias = blocks.transpose(1, 0, 2, 3).reshape(HEADS, NTOK, NTOK)
    queries = projected[0].reshape(NTOK, HEADS, HEAD).astype(jnp.float32)
    key_rows = projected[1].reshape(NTOK, HEADS, HEAD).astype(jnp.float32)
    val_rows = projected[2].reshape(NTOK, HEADS, HEAD).astype(jnp.float32)
    scores = jnp.einsum('ihd,jhd->hij', queries, key_rows) / jnp.sqrt(jnp.float32(HEAD)) + pair_bias
    token_index = jnp.arange(NTOK, dtype=jnp.int32)
    allowed = (token_mask[None, :] == 1) | (token_index[:, None] == token_index[None, :])
    scores = jnp.where(allowed[None], scores, NEGATIVE)
    row_top = lax.optimization_barrier(jnp.max(scores, axis=-1, keepdims=True))
    weights = jnp.where(allowed[None], jnp.exp(scores - row_top), 0.0)
    totals = lax.optimization_barrier(jnp.sum(weights, axis=-1))
    weighted = jnp.einsum('hij,jhd->ihd', weights.astype(jnp.bfloat16).astype(jnp.float32), val_rows)
    attended = weighted / totals.T[:, :, None]
    gate_rows = jax.nn.sigmoid(projected[3].astype(jnp.float32)).reshape(NTOK, HEADS, HEAD)
    token_out = (gate_rows * attended).reshape(NTOK, HEADS * HEAD).astype(jnp.bfloat16)
    return (atom_out, token_out)
```

```python
import functools

import jax
import jax.numpy as jnp
from jax import lax
from jax.experimental import pallas as pl
from jax.experimental.pallas import tpu as pltpu
from jax.sharding import PartitionSpec as P

ATOM_HEADS = 4
ATOM_BLOCKS = 3
QWIN = 32
KWIN = 128
TRANS = 2
MARGIN = (KWIN - QWIN) // 2
HALO_FEATS = 3
HALO_BIAS = 2

EPSILON = 1e-05
NEGATIVE = -1e30


VMEM = pl.BlockSpec(memory_space=pltpu.VMEM)
SMEM = pl.BlockSpec(memory_space=pltpu.SMEM)
F32 = jnp.float32
BF16 = jnp.bfloat16


def nt(a, b):
    return lax.dot_general(a, b, (((1,), (1,)), ((), ())), preferred_element_type=F32)


def tn(a, b):
    return lax.dot_general(a, b, (((0,), (0,)), ((), ())), preferred_element_type=F32)


def mm(a, b):
    return jnp.dot(a, b, preferred_element_type=F32)


def norm_rows(x, gain):
    average = jnp.mean(x, axis=-1, keepdims=True)
    centered = x - average
    variance = jnp.mean(centered * centered, axis=-1, keepdims=True)
    return centered * lax.rsqrt(variance + EPSILON) * gain


def sigmoid(x):
    return 1.0 / (1.0 + jnp.exp(-x))


def call(body, out_shape, n_smem, n_vmem, scratch=(), flops=0, nbytes=0, name=None, vmem=None):
    return pl.pallas_call(
        body,
        out_shape=out_shape,
        in_specs=[SMEM] * n_smem + [VMEM] * n_vmem,
        out_specs=jax.tree.map(lambda _: VMEM, out_shape),
        scratch_shapes=list(scratch),
        cost_estimate=pl.CostEstimate(flops=flops, bytes_accessed=nbytes, transcendentals=0),
        compiler_params=pltpu.CompilerParams(vmem_limit_bytes=vmem) if vmem else None,
        name=name,
    )


def pack_body(total_atoms, pos, bias, mask, feats, out):
    rows = feats.shape[0]
    out[0] = feats[...]
    slot = lax.broadcasted_iota(jnp.int32, (1, KWIN), 1)
    own = (slot >= MARGIN) & (slot < MARGIN + QWIN)
    for w in range(rows // QWIN):
        index = pos[0] + w * QWIN - MARGIN + slot
        usable = ((index >= 0) & (index < total_atoms) & (mask[pl.ds(w, 1), :] == 1)) | own
        keep = jnp.broadcast_to(usable, (QWIN, KWIN))
        for h in range(ATOM_HEADS):
            part = bias[h, w * QWIN : (w + 1) * QWIN, :].astype(F32)
            out[1 + h, w * QWIN : (w + 1) * QWIN, :] = jnp.where(keep, part, NEGATIVE).astype(BF16)


def ends_body(n_col, pos, *refs):
    pieces, (left, right) = refs[:n_col], refs[n_col:]
    planes = ATOM_HEADS
    for k in range(n_col):
        at = lax.rem(pos[0] + (n_col - k), n_col)
        back = at - (n_col - HALO_FEATS)

        @pl.when(at < HALO_FEATS)
        def _():
            left[pl.ds(at, 1)] = pieces[k][0:1]

        @pl.when(at < HALO_BIAS)
        def _():
            left[pl.ds(HALO_FEATS + planes * at, planes)] = pieces[k][1:]

        @pl.when(back >= 0)
        def _():
            right[pl.ds(back, 1)] = pieces[k][0:1]

        @pl.when(back >= HALO_FEATS - HALO_BIAS)
        def _():
            spot = HALO_FEATS + planes * (back - (HALO_FEATS - HALO_BIAS))
            right[pl.ds(spot, planes)] = pieces[k][1:]


def atom_body(n_col, pos, *refs):
    pieces = refs[:n_col]
    low, high, norms, w_qkv, w_gate, w_out, w_up, w_down, row_out, own_out = refs[n_col : n_col + 10]
    state, bias, normed_s, keys_s, vals_s, query_s, att_s = refs[n_col + 10 :]
    rows, width = own_out.shape
    group = row_out.shape[0]
    head = width // ATOM_HEADS
    ext = HALO_FEATS * rows
    bext = HALO_BIAS * rows
    for t in range(HALO_FEATS):
        state[t * rows : (t + 1) * rows] = low[t].astype(F32)
        state[ext + group + t * rows : ext + group + (t + 1) * rows] = high[t].astype(F32)
    for t in range(HALO_BIAS):
        for h in range(ATOM_HEADS):
            plane = HALO_FEATS + t * ATOM_HEADS + h
            bias[h, t * rows : (t + 1) * rows] = low[plane]
            bias[h, bext + group + t * rows : bext + group + (t + 1) * rows] = high[plane]
    for k in range(n_col):
        at = lax.rem(pos[0] + (n_col - k), n_col) * rows
        state[pl.ds(pl.multiple_of(ext + at, rows), rows)] = pieces[k][0].astype(F32)
        for h in range(ATOM_HEADS):
            bias[h, pl.ds(pl.multiple_of(bext + at, rows), rows)] = pieces[k][1 + h]
    lane = lax.broadcasted_iota(jnp.int32, (1, width), 1)
    scale = 1.0 / (head**0.5)
    for block in range(ATOM_BLOCKS):
        rest = (ATOM_BLOCKS - 1 - block) * rows
        count = group + 2 * rest
        first = ext - rest
        base = first - MARGIN
        span = count + 2 * MARGIN
        bias_at = bext - rest
        gain = norms[block, 0:1]
        normed = norm_rows(state[base : base + span], gain).astype(BF16)
        normed_s[0:span] = normed
        qkv = mm(normed, w_qkv[block])
        query_s[0:span] = qkv[:, :width].astype(BF16)
        keys_s[0:span] = qkv[:, width : 2 * width].astype(BF16)
        vals_s[0:span] = qkv[:, 2 * width :].astype(BF16)

        def window(at):
            query = query_s[pl.ds(at + MARGIN, QWIN)]
            spread = jnp.concatenate(
                [jnp.where(lane // head == h, query, jnp.zeros_like(query)) for h in range(ATOM_HEADS)],
                axis=0,
            )
            key = keys_s[pl.ds(at, KWIN)]
            val = vals_s[pl.ds(at, KWIN)]
            extra = bias[:, pl.ds(bias_at + at, QWIN), :].astype(F32)
            scores = nt(spread, key) * scale + extra.reshape(ATOM_HEADS * QWIN, KWIN)
            top = jnp.max(scores, axis=-1, keepdims=True)
            weights = jnp.exp(scores - top)
            total = jnp.sum(weights, axis=-1, keepdims=True)
            mixed = mm(weights.astype(BF16), val) * (1.0 / total)
            attended = jnp.zeros((QWIN, width), F32)
            for h in range(ATOM_HEADS):
                attended = jnp.where(lane // head == h, mixed[h * QWIN : (h + 1) * QWIN], attended)
            att_s[pl.ds(at, QWIN)] = attended

        n_win = count // QWIN
        if n_win <= 16:
            for w in range(n_win):
                window(w * QWIN)
        else:

            def several(step, carry):
                for w in range(4):
                    window(pl.multiple_of((step * 4 + w) * QWIN, QWIN))
                return carry

            lax.fori_loop(0, n_win // 4, several, 0)
        gates = sigmoid(mm(normed_s[MARGIN : MARGIN + count], w_gate[block]))
        mixed = (gates * att_s[0:count]).astype(BF16)
        now = state[first : first + count] + mm(mixed, w_out[block])
        normed_two = norm_rows(now, norms[block, 1:2]).astype(BF16)
        both = mm(normed_two, w_up[block])
        half = both.shape[1] // 2
        gate_half = both[:, :half]
        hidden = (gate_half * sigmoid(gate_half) * both[:, half:]).astype(BF16)
        state[first : first + count] = now + mm(hidden, w_down[block])
    row_out[...] = state[ext : ext + group].astype(BF16)
    own = pl.multiple_of(ext + pos[0] * rows, rows)
    own_out[...] = state[pl.ds(own, rows)].astype(BF16)


def pair_body(chunk, pos, live, pair, norms, w_up, w_down, w_bias, out):
    tile_q, tile_k, width = pair.shape
    heads = w_bias.shape[0]
    group = 128 // heads
    half = w_up.shape[2] // 2
    tall = jnp.concatenate([w_bias[...]] * group, axis=0)
    high = tall.astype(BF16)
    low = (tall - high.astype(F32)).astype(BF16)
    spread = jnp.concatenate(
        [jnp.concatenate([high, high], axis=1), jnp.concatenate([low, low], axis=1)], axis=0
    )
    lane = lax.broadcasted_iota(jnp.int32, (1, 128), 1)
    n_tok = live.shape[1]
    key_at = pos[1] + lax.broadcasted_iota(jnp.int32, (tile_k, n_tok), 0)
    spots = lax.broadcasted_iota(jnp.int32, (tile_k, n_tok), 1)
    seen = jnp.where(key_at == spots, live[...], 0).astype(F32)
    alive = jnp.sum(seen, axis=-1, keepdims=True) == 1.0
    key_index = pos[1] + lax.broadcasted_iota(jnp.int32, (tile_k, 128), 0)
    lane_full = lax.broadcasted_iota(jnp.int32, (tile_k, 128), 1)
    for g in range(tile_q // group):
        acc = jnp.zeros((tile_k, 128), F32)
        for sub in range(group // chunk):
            start = g * group + sub * chunk
            z = pair[start : start + chunk].astype(F32).reshape(chunk * tile_k, width)
            for m in range(TRANS):
                normed = norm_rows(z, norms[m : m + 1]).astype(BF16)
                both = mm(normed, w_up[m])
                first = both[:, :half]
                hidden = (first * sigmoid(first) * both[:, half:]).astype(BF16)
                z = z + mm(hidden, w_down[m])
            final = norm_rows(z, norms[TRANS : TRANS + 1])
            final_high = final.astype(BF16)
            final_low = (final - final_high.astype(F32)).astype(BF16)
            wide = mm_wide = nt(jnp.concatenate([final_high, final_low], axis=1), spread)
            summed = wide[:, :128] + mm_wide[:, 128:]
            for i in range(chunk):
                acc = jnp.where(lane // heads == sub * chunk + i, summed[i * tile_k : (i + 1) * tile_k], acc)
        query_index = pos[0] + g * group + lane_full // heads
        allowed = alive | (query_index == key_index)
        out[:, g * 128 : (g + 1) * 128] = jnp.where(allowed, acc, NEGATIVE)


def token_body(n_row, n_col, tile, heads, pos, *refs):
    groups, tiles = refs[:n_row], refs[n_row : n_row + n_col]
    ids, w_agg, gain, w_token, out = refs[n_row + n_col : n_row + n_col + 5]
    atoms, feat, sums, counts, tokens, keys, vals, bias = refs[n_row + n_col + 5 :]
    group = groups[0].shape[0]
    n_tok = sums.shape[0]
    for k in range(n_row):
        at = lax.rem(pos[0] + (n_row - k), n_row) * group
        atoms[pl.ds(pl.multiple_of(at, group), group)] = groups[k][...]
    for k in range(n_col):
        at = lax.rem(pos[1] + (n_col - k), n_col) * tile
        bias[pl.ds(pl.multiple_of(at, tile), tile)] = tiles[k][...]
    size = feat.shape[0]
    steps = atoms.shape[0] // size
    token = lax.broadcasted_iota(jnp.int32, (n_tok, size), 0)

    def gathered(step):
        at = step * size if steps == 1 else pl.multiple_of(step * size, size)
        some = atoms[pl.ds(at, size)]
        feat[...] = jnp.maximum(mm(some, w_agg[...]), 0.0).astype(BF16)
        hot = jnp.where(token == ids[pl.ds(step, 1), :], 1.0, 0.0)
        return mm(hot.astype(BF16), feat[...]), jnp.sum(hot, axis=-1, keepdims=True)

    if steps == 1:
        total, number = gathered(0)
    else:
        sums[...] = jnp.zeros_like(sums)
        counts[...] = jnp.zeros_like(counts)

        def more(step, carry):
            part, some = gathered(step)
            sums[...] += part
            counts[...] += jnp.broadcast_to(some, counts.shape)
            return carry

        lax.fori_loop(0, steps, more, 0)
        total, number = sums[...], counts[:, 0:1]
    tokens[...] = norm_rows(total * (1.0 / number), gain[...]).astype(BF16)
    keys[...] = mm(tokens[...], w_token[1]).astype(BF16)
    vals[...] = mm(tokens[...], w_token[2]).astype(BF16)
    mine = tokens[pl.ds(pl.multiple_of(pos[0] * tile, tile), tile)]
    query = mm(mine, w_token[0]).astype(BF16).astype(F32)
    gates = sigmoid(mm(mine, w_token[3]).astype(BF16).astype(F32))
    width = query.shape[1]
    head = width // heads
    lane = lax.broadcasted_iota(jnp.int32, (heads, width), 1)
    which = lax.broadcasted_iota(jnp.int32, (heads, width), 0)
    own = (lane >= which * head) & (lane < (which + 1) * head)
    own = jnp.broadcast_to(own[None], (tile, heads, width))
    spread = jnp.where(own, query[:, None, :], 0.0).reshape(tile * heads, width).astype(BF16)
    scores = nt(keys[...], spread) * (1.0 / head**0.5) + bias[...]
    top = jnp.max(scores, axis=0, keepdims=True)
    weights = jnp.exp(scores - top)
    total_w = jnp.sum(weights, axis=0, keepdims=True)
    mixed = tn(weights.astype(BF16), vals[...])
    inverse = jnp.transpose(jnp.broadcast_to(1.0 / total_w, (8, tile * heads)))[:, 0:1]
    mixed = (mixed * inverse).reshape(tile, heads, width)
    attended = jnp.sum(jnp.where(own, mixed, 0.0), axis=1)
    out[...] = (gates * attended).astype(BF16)


def ring_gather(value, axis):
    count = lax.axis_size(axis)
    return [value] + [
        lax.ppermute(value, axis, [(i, (i + k) % count) for i in range(count)]) for k in range(1, count)
    ]


def per_device(
    atom_feats,
    atom_bias,
    key_mask,
    atom_token,
    token_mask,
    pair,
    atom_norms,
    w_atom_qkv,
    w_atom_gate,
    w_atom_out,
    w_atom_up,
    w_atom_down,
    w_agg,
    token_norm,
    w_token,
    pair_norms,
    w_pair_up,
    w_pair_down,
    w_bias,
):
    rows, width = atom_feats.shape
    n_row, n_col = lax.axis_size("row"), lax.axis_size("col")
    row, col = lax.axis_index("row").astype(jnp.int32), lax.axis_index("col").astype(jnp.int32)
    n_tok = token_mask.shape[0]
    tile = pair.shape[0]
    heads = w_bias.shape[1]
    planes = 1 + ATOM_HEADS
    group = rows * n_col
    shape = jax.ShapeDtypeStruct

    first = ((row * n_col + col) * rows).reshape(1)
    packed = call(
        functools.partial(pack_body, group * n_row),
        shape((planes, rows, width), BF16),
        1,
        3,
        name="pack",
        nbytes=2 * planes * rows * width * 2,
    )(first, atom_bias, key_mask, atom_feats)
    pieces = ring_gather(packed, "col")

    tile_at = jnp.stack([row * tile, col * tile])
    pair_out = call(
        functools.partial(pair_body, 8),
        shape((pair.shape[1], tile * heads), F32),
        1,
        6,
        name="pair",
        flops=2 * pair.size * w_pair_up.shape[2] * 3,
        nbytes=2 * (pair.size + w_pair_up.size + w_pair_down.size),
    )(tile_at, token_mask.reshape(1, -1), pair, pair_norms, w_pair_up, w_pair_down, w_bias.T)

    halo = HALO_FEATS + ATOM_HEADS * HALO_BIAS
    col_at = col.reshape(1)
    left, right = call(
        functools.partial(ends_body, n_col),
        [shape((halo, rows, width), BF16)] * 2,
        1,
        n_col,
        name="ends",
        nbytes=4 * halo * rows * width * 2,
    )(col_at, *pieces)
    low = lax.ppermute(right, "row", [(i, (i + 1) % n_row) for i in range(n_row)])
    high = lax.ppermute(left, "row", [(i, (i - 1) % n_row) for i in range(n_row)])
    tiles = ring_gather(pair_out, "col")

    region = group + 2 * HALO_FEATS * rows
    row_out, atom_out = call(
        functools.partial(atom_body, n_col),
        [shape((group, width), BF16), shape((rows, width), BF16)],
        1,
        n_col + 8,
        scratch=[
            pltpu.VMEM((region, width), F32),
            pltpu.VMEM((ATOM_HEADS, group + 2 * HALO_BIAS * rows, KWIN), BF16),
            pltpu.VMEM((region, width), BF16),
            pltpu.VMEM((region, width), BF16),
            pltpu.VMEM((region, width), BF16),
            pltpu.VMEM((region, width), BF16),
            pltpu.VMEM((region, width), F32),
        ],
        name="atoms",
        flops=6 * region * width * width * 2 * 10,
        nbytes=4 * region * width * 2,
    )(col_at, *pieces, low, high, atom_norms, w_atom_qkv, w_atom_gate, w_atom_out, w_atom_up, w_atom_down)
    groups = ring_gather(row_out, "row")

    total = group * n_row
    size = min(total, 1024)
    channels = w_agg.shape[1]
    token_out = call(
        functools.partial(token_body, n_row, n_col, tile, heads),
        shape((tile, w_token.shape[2]), BF16),
        1,
        n_row + n_col + 4,
        scratch=[
            pltpu.VMEM((total, width), BF16),
            pltpu.VMEM((size, channels), BF16),
            pltpu.VMEM((n_tok, channels), F32),
            pltpu.VMEM((n_tok, 128), F32),
            pltpu.VMEM((n_tok, channels), BF16),
            pltpu.VMEM((n_tok, w_token.shape[2]), BF16),
            pltpu.VMEM((n_tok, w_token.shape[2]), BF16),
            pltpu.VMEM((n_tok, tile * heads), F32),
        ],
        name="tokens",
        flops=2 * total * width * channels,
        nbytes=2 * w_token.size,
    )(
        jnp.stack([row, col]),
        *groups,
        *tiles,
        atom_token.reshape(-1, size),
        w_agg,
        token_norm.reshape(1, -1),
        w_token,
    )
    return (atom_out, token_out)


def solution(mesh):
    placed = (
        P(("parts", "row", "col"), None),
        P(None, ("parts", "row", "col"), None),
        P(("parts", "row", "col"), None),
        P("parts"),
        P("parts"),
        P(("parts", "row"), "col", None),
    ) + (P(),) * 13
    return jax.shard_map(
        per_device,
        mesh=mesh,
        in_specs=placed,
        out_specs=(P(("parts", "row", "col"), None), P(("parts", "row"), None)),
        check_vma=False,
    )
```

```python
import functools

import jax
import jax.numpy as jnp
from jax import lax
from jax.experimental import pallas as pl
from jax.experimental.pallas import tpu as pltpu
from jax.sharding import PartitionSpec as P

ATOM_HEADS = 4
ATOM_BLOCKS = 3
QWIN = 32
KWIN = 128
TRANS = 2
MARGIN = (KWIN - QWIN) // 2
HALO_FEATS = 3
HALO_BIAS = 2

EPSILON = 1e-05
NEGATIVE = -1e30


VMEM = pl.BlockSpec(memory_space=pltpu.VMEM)
SMEM = pl.BlockSpec(memory_space=pltpu.SMEM)
HBM = pl.BlockSpec(memory_space=pltpu.HBM)
F32 = jnp.float32
BF16 = jnp.bfloat16


def nt(a, b):
    return lax.dot_general(a, b, (((1,), (1,)), ((), ())), preferred_element_type=F32)


def tn(a, b):
    return lax.dot_general(a, b, (((0,), (0,)), ((), ())), preferred_element_type=F32)


def mm(a, b):
    return jnp.dot(a, b, preferred_element_type=F32)


def norm_rows(x, gain):
    average = jnp.mean(x, axis=-1, keepdims=True)
    centered = x - average
    variance = jnp.mean(centered * centered, axis=-1, keepdims=True)
    return centered * lax.rsqrt(variance + EPSILON) * gain


def norm_wide(x, gain, ones):
    centered = x - jnp.mean(x, axis=-1, keepdims=True)
    squares = centered * centered
    high = squares.astype(BF16)
    low = (squares - high.astype(F32)).astype(BF16)
    variance = mm(jnp.concatenate([high, low], axis=1), ones)
    return centered * lax.rsqrt(variance + EPSILON) * gain


def sigmoid(x):
    return 0.5 * jnp.tanh(0.5 * x) + 0.5


def gated(first, second):
    half = 0.5 * first
    return ((half * jnp.tanh(half) + half) * second).astype(BF16)


def call(body, out_shape, n_smem, n_vmem, scratch=(), flops=0, nbytes=0, name=None, vmem=None):
    return pl.pallas_call(
        body,
        out_shape=out_shape,
        in_specs=[SMEM] * n_smem + [VMEM] * n_vmem,
        out_specs=jax.tree.map(lambda _: VMEM, out_shape),
        scratch_shapes=list(scratch),
        cost_estimate=pl.CostEstimate(flops=flops, bytes_accessed=nbytes, transcendentals=0),
        compiler_params=pltpu.CompilerParams(vmem_limit_bytes=vmem) if vmem else None,
        name=name,
    )


def pack_body(n_row, n_col, n_load, row, col, bias, mask, feats, *refs):
    loads, out, loaded = refs[:n_load], refs[n_load], refs[n_load + 1 : 2 * n_load + 1]
    bias_v, mask_v, sems = refs[2 * n_load + 1 :]
    rows = feats.shape[0]
    copies = [
        pltpu.make_async_copy(source, target, sems.at[i])
        for i, (source, target) in enumerate(
            ((mask, mask_v), (bias, bias_v), (feats, out.at[0 : rows]), *zip(loads, loaded))
        )
    ]
    for copy in copies:
        copy.start()
    for copy in copies[:3]:
        copy.wait()
    total_atoms = n_row * n_col * rows
    begin = (row[0] * n_col + col[0]) * rows
    slot = lax.broadcasted_iota(jnp.int32, (1, KWIN), 1)
    own = (slot >= MARGIN) & (slot < MARGIN + QWIN)
    for w in range(rows // QWIN):
        index = begin + w * QWIN - MARGIN + slot
        usable = ((index >= 0) & (index < total_atoms) & (mask_v[w : w + 1, :] == 1)) | own
        keep = jnp.broadcast_to(usable, (QWIN, KWIN))
        for h in range(ATOM_HEADS):
            part = bias_v[h, w * QWIN : (w + 1) * QWIN, :].astype(F32)
            at = rows + (w * ATOM_HEADS + h) * QWIN
            out[at : at + QWIN, :] = jnp.where(keep, part, NEGATIVE).astype(BF16)
    for copy in copies[3:]:
        copy.wait()


def ends_body(n_col, rows, col, *refs):
    pieces, (left, right) = refs[:n_col], refs[n_col:]
    feats, fat = HALO_FEATS * rows, ATOM_HEADS * rows
    for k in range(n_col):
        at = col[0] ^ k
        back = at - (n_col - HALO_FEATS)

        @pl.when(at < HALO_FEATS)
        def _():
            left[pl.ds(pl.multiple_of(at * rows, rows), rows)] = pieces[k][0:rows]

        @pl.when(at < HALO_BIAS)
        def _():
            left[pl.ds(pl.multiple_of(feats + at * fat, rows), fat)] = pieces[k][rows:]

        @pl.when(back >= 0)
        def _():
            right[pl.ds(pl.multiple_of(back * rows, rows), rows)] = pieces[k][0:rows]

        @pl.when(back >= HALO_FEATS - HALO_BIAS)
        def _():
            spot = feats + (back - (HALO_FEATS - HALO_BIAS)) * fat
            right[pl.ds(pl.multiple_of(spot, rows), fat)] = pieces[k][rows:]


def atom_body(n_col, together, col, *refs):
    pieces = refs[:n_col]
    low, high, norms, w_qkv, w_gate, w_out, w_up, w_down, row_out, own_out = refs[n_col : n_col + 10]
    state, bias, normed_s, keys_s, vals_s, query_s, att_s = refs[n_col + 10 :]
    rows, width = own_out.shape
    group = row_out.shape[0]
    head = width // ATOM_HEADS
    ext = HALO_FEATS * rows
    bext = HALO_BIAS * rows
    fat = ATOM_HEADS * rows
    state[0:ext] = low[0:ext].astype(F32)
    state[ext + group : 2 * ext + group] = high[0:ext].astype(F32)
    bias[0 : HALO_BIAS * fat] = low[ext : ext + HALO_BIAS * fat]
    after = (bext + group) * ATOM_HEADS
    bias[after : after + HALO_BIAS * fat] = high[ext : ext + HALO_BIAS * fat]
    for k in range(n_col):
        at = (col[0] ^ k) * rows
        state[pl.ds(pl.multiple_of(ext + at, rows), rows)] = pieces[k][0:rows].astype(F32)
        bias[pl.ds(pl.multiple_of((bext + at) * ATOM_HEADS, rows), fat)] = pieces[k][rows:]
    ones = jnp.full((2 * width, width), 1.0 / width, BF16)
    lane = lax.broadcasted_iota(jnp.int32, (1, width), 1)
    scale = 1.0 / (head**0.5)
    tall = ATOM_HEADS * QWIN
    for block in range(ATOM_BLOCKS):
        rest = (ATOM_BLOCKS - 1 - block) * rows
        count = group + 2 * rest
        first = ext - rest
        base = first - MARGIN
        span = count + 2 * MARGIN
        bias_at = (bext - rest) * ATOM_HEADS
        normed = norm_wide(state[base : base + span], norms[block, 0:1], ones).astype(BF16)
        normed_s[0:span] = normed
        qkv = mm(normed, w_qkv[block])
        query_s[0:span] = qkv[:, :width].astype(BF16)
        keys_s[0:span] = qkv[:, width : 2 * width].astype(BF16)
        vals_s[0:span] = qkv[:, 2 * width :].astype(BF16)
        n_win = count // QWIN
        for start in range(0, n_win, together):
            spots = [w * QWIN for w in range(start, min(start + together, n_win))]
            parts = []
            for at in spots:
                query = query_s[at + MARGIN : at + MARGIN + QWIN]
                spread = jnp.concatenate(
                    [jnp.where(lane // head == h, query, jnp.zeros_like(query)) for h in range(ATOM_HEADS)],
                    axis=0,
                )
                parts.append(nt(spread, keys_s[at : at + KWIN]))
            bias_row = bias_at + start * tall
            extra = bias[bias_row : bias_row + len(spots) * tall].astype(F32)
            scores = jnp.concatenate(parts, axis=0) * scale + extra
            weights = jnp.exp(scores - jnp.max(scores, axis=-1, keepdims=True))
            totals = jnp.sum(weights, axis=-1, keepdims=True)
            weights = weights.astype(BF16)
            for i, at in enumerate(spots):
                mixed = mm(weights[i * tall : (i + 1) * tall], vals_s[at : at + KWIN])
                total = jnp.broadcast_to(totals[i * tall : (i + 1) * tall], (tall, width))
                weighted, divisor = mixed[:QWIN], total[:QWIN]
                for h in range(1, ATOM_HEADS):
                    mine = lane // head == h
                    weighted = jnp.where(mine, mixed[h * QWIN : (h + 1) * QWIN], weighted)
                    divisor = jnp.where(mine, total[h * QWIN : (h + 1) * QWIN], divisor)
                att_s[at : at + QWIN] = weighted / divisor
        gates = sigmoid(mm(normed_s[MARGIN : MARGIN + count], w_gate[block]))
        mixed = (gates * att_s[0:count]).astype(BF16)
        now = state[first : first + count] + mm(mixed, w_out[block])
        normed_two = norm_wide(now, norms[block, 1:2], ones).astype(BF16)
        both = mm(normed_two, w_up[block])
        half = both.shape[1] // 2
        hidden = gated(both[:, :half], both[:, half:])
        state[first : first + count] = now + mm(hidden, w_down[block])
    row_out[...] = state[ext : ext + group].astype(BF16)
    own = pl.multiple_of(ext + col[0] * rows, rows)
    own_out[...] = state[pl.ds(own, rows)].astype(BF16)


def pair_body(begin, end, row, col, live, pair, norms, w_up, w_down, w_bias, *refs):
    earlier, out = refs[:-1], refs[-1]
    _, tile_k, width = pair.shape
    tile_q = pair.shape[0]
    heads = w_bias.shape[0]
    group = 128 // heads
    half = w_up.shape[2] // 2
    ones = jnp.full((2 * width, width), 1.0 / width, BF16)
    tall = jnp.concatenate([w_bias[...]] * group, axis=0)
    high = tall.astype(BF16)
    low = (tall - high.astype(F32)).astype(BF16)
    spread = jnp.concatenate(
        [jnp.concatenate([high, high], axis=1), jnp.concatenate([low, low], axis=1)], axis=0
    )
    lane = lax.broadcasted_iota(jnp.int32, (1, 128), 1)
    n_tok = live.shape[1]
    key_at = col[0] * tile_k + lax.broadcasted_iota(jnp.int32, (tile_k, n_tok), 0)
    spots = lax.broadcasted_iota(jnp.int32, (tile_k, n_tok), 1)
    seen = jnp.where(key_at == spots, live[...], 0).astype(F32)
    alive = jnp.sum(seen, axis=-1, keepdims=True) == 1.0
    key_index = col[0] * tile_k + lax.broadcasted_iota(jnp.int32, (tile_k, 128), 0)
    lane_full = lax.broadcasted_iota(jnp.int32, (tile_k, 128), 1)
    if earlier:
        done = begin // group * 128
        out[:, :done] = earlier[0][...]
    else:
        done = 0
    z = pair[begin:end].astype(F32).reshape((end - begin) * tile_k, width)
    for m in range(TRANS):
        normed = norm_wide(z, norms[m : m + 1], ones).astype(BF16)
        both = mm(normed, w_up[m])
        z = z + mm(gated(both[:, :half], both[:, half:]), w_down[m])
    final = norm_wide(z, norms[TRANS : TRANS + 1], ones)
    final_high = final.astype(BF16)
    final_low = (final - final_high.astype(F32)).astype(BF16)
    wide = nt(jnp.concatenate([final_high, final_low], axis=1), spread)
    summed = wide[:, :128] + wide[:, 128:]
    for g in range((end - begin) // group):
        acc = jnp.zeros((tile_k, 128), F32)
        for i in range(group):
            at = (g * group + i) * tile_k
            acc = jnp.where(lane // heads == i, summed[at : at + tile_k], acc)
        query_index = row[0] * tile_q + begin + g * group + lane_full // heads
        allowed = alive | (query_index == key_index)
        out[:, done + g * 128 : done + (g + 1) * 128] = jnp.where(allowed, acc, NEGATIVE)


def token_body(n_row, n_col, tile, heads, row, col, *refs):
    groups, tiles = refs[:n_row], refs[n_row : n_row + n_col]
    ids, w_agg, gain, w_token, out = refs[n_row + n_col : n_row + n_col + 5]
    atoms, feat, sums, counts, tokens, keys, vals, bias = refs[n_row + n_col + 5 :]
    group = groups[0].shape[0]
    n_tok = sums.shape[0]
    for k in range(n_row):
        at = lax.rem(row[0] + (n_row - k), n_row) * group
        atoms[pl.ds(pl.multiple_of(at, group), group)] = groups[k][...]
    for k in range(n_col):
        at = (col[0] ^ k) * tile
        bias[pl.ds(pl.multiple_of(at, tile), tile)] = tiles[k][...]
    size = feat.shape[0]
    steps = atoms.shape[0] // size
    token = lax.broadcasted_iota(jnp.int32, (n_tok, size), 0)

    def gathered(step):
        at = step * size if steps == 1 else pl.multiple_of(step * size, size)
        some = atoms[pl.ds(at, size)]
        feat[...] = jnp.maximum(mm(some, w_agg[...]), 0.0).astype(BF16)
        hot = jnp.where(token == ids[pl.ds(step, 1), :], 1.0, 0.0)
        return mm(hot.astype(BF16), feat[...]), jnp.sum(hot, axis=-1, keepdims=True)

    if steps == 1:
        total, number = gathered(0)
    else:
        sums[...] = jnp.zeros_like(sums)
        counts[...] = jnp.zeros_like(counts)

        def more(step, carry):
            part, some = gathered(step)
            sums[...] += part
            counts[...] += jnp.broadcast_to(some, counts.shape)
            return carry

        lax.fori_loop(0, steps, more, 0)
        total, number = sums[...], counts[:, 0:1]
    tokens[...] = norm_rows(total * (1.0 / number), gain[...]).astype(BF16)
    keys[...] = mm(tokens[...], w_token[1]).astype(BF16)
    vals[...] = mm(tokens[...], w_token[2]).astype(BF16)
    mine = tokens[pl.ds(pl.multiple_of(row[0] * tile, tile), tile)]
    query = mm(mine, w_token[0]).astype(BF16).astype(F32)
    gates = sigmoid(mm(mine, w_token[3]).astype(BF16).astype(F32))
    width = query.shape[1]
    head = width // heads
    lane = lax.broadcasted_iota(jnp.int32, (heads, width), 1)
    which = lax.broadcasted_iota(jnp.int32, (heads, width), 0)
    own = (lane >= which * head) & (lane < (which + 1) * head)
    own = jnp.broadcast_to(own[None], (tile, heads, width))
    spread = jnp.where(own, query[:, None, :], 0.0).reshape(tile * heads, width).astype(BF16)
    scores = nt(keys[...], spread) * (1.0 / head**0.5) + bias[...]
    top = jnp.max(scores, axis=0, keepdims=True)
    weights = jnp.exp(scores - top)
    total_w = jnp.sum(weights, axis=0, keepdims=True)
    mixed = tn(weights.astype(BF16), vals[...])
    inverse = jnp.transpose(jnp.broadcast_to(1.0 / total_w, (8, tile * heads)))[:, 0:1]
    mixed = (mixed * inverse).reshape(tile, heads, width)
    attended = jnp.sum(jnp.where(own, mixed, 0.0), axis=1)
    out[...] = (gates * attended).astype(BF16)


def in_hbm(value):
    return pltpu.with_memory_space_constraint(value, pltpu.HBM)


def gather(value, axis, partner):
    count = lax.axis_size(axis)
    return [value] + [
        lax.ppermute(value, axis, [(i, partner(i, k, count)) for i in range(count)]) for k in range(1, count)
    ]


def ring(i, k, count):
    return (i + k) % count


def swap(i, k, count):
    return i ^ k


def per_device(
    atom_feats,
    atom_bias,
    key_mask,
    atom_token,
    token_mask,
    pair,
    atom_norms,
    w_atom_qkv,
    w_atom_gate,
    w_atom_out,
    w_atom_up,
    w_atom_down,
    w_agg,
    token_norm,
    w_token,
    pair_norms,
    w_pair_up,
    w_pair_down,
    w_bias,
):
    rows, width = atom_feats.shape
    n_row, n_col = lax.axis_size("row"), lax.axis_size("col")
    row, col = lax.axis_index("row").astype(jnp.int32), lax.axis_index("col").astype(jnp.int32)
    n_tok = token_mask.shape[0]
    tile = pair.shape[0]
    heads = w_bias.shape[1]
    planes = 1 + ATOM_HEADS
    group = rows * n_col
    shape = jax.ShapeDtypeStruct

    row_at, col_at = row.reshape(1), col.reshape(1)
    assert n_col & (n_col - 1) == 0 and n_col >= HALO_FEATS
    for_pair = (token_mask.reshape(1, -1), pair, pair_norms, w_pair_up, w_pair_down, w_bias.T)
    n_load = len(for_pair)
    packed, *for_pair = pl.pallas_call(
        functools.partial(pack_body, n_row, n_col, n_load),
        out_shape=[shape((planes * rows, width), BF16)] + [shape(x.shape, x.dtype) for x in for_pair],
        in_specs=[SMEM] * 2 + [HBM] * (3 + n_load),
        out_specs=[VMEM] * (1 + n_load),
        scratch_shapes=[
            pltpu.VMEM(atom_bias.shape, BF16),
            pltpu.VMEM(key_mask.shape, jnp.int32),
            pltpu.SemaphoreType.DMA((3 + n_load,)),
        ],
        compiler_params=pltpu.CompilerParams(vmem_limit_bytes=8 << 20),
        name="pack",
    )(row_at, col_at, *map(in_hbm, (atom_bias, key_mask, atom_feats, *for_pair)))
    pieces = gather(packed, "col", swap)

    def pair_part(begin, end, *earlier):
        return call(
            functools.partial(pair_body, begin, end),
            shape((pair.shape[1], end * heads), F32),
            2,
            n_load + len(earlier),
            name="pair",
            vmem=24 << 20,
            flops=2 * (end - begin) * pair.shape[1] * pair.shape[2] * w_pair_up.shape[2] * 3,
        )(row_at, col_at, *for_pair, *earlier)

    split = (tile * heads // 128 * 2 // 3) * 128 // heads
    pair_out = pair_part(0, split)
    *pieces, pair_out = lax.optimization_barrier((*pieces, pair_out))
    halo = (HALO_FEATS + ATOM_HEADS * HALO_BIAS) * rows
    left, right = call(
        functools.partial(ends_body, n_col, rows),
        [shape((halo, width), BF16)] * 2,
        1,
        n_col,
        name="ends",
        vmem=8 << 20,
    )(col_at, *pieces)
    low = lax.ppermute(right, "row", [(i, (i + 1) % n_row) for i in range(n_row)])
    high = lax.ppermute(left, "row", [(i, (i - 1) % n_row) for i in range(n_row)])
    pair_out, left, right = lax.optimization_barrier((pair_out, left, right))
    pair_out = pair_part(split, tile, pair_out)
    low, high, pair_out = lax.optimization_barrier((low, high, pair_out))
    tiles = gather(pair_out, "col", swap)

    region = group + 2 * HALO_FEATS * rows
    row_out, atom_out = call(
        functools.partial(atom_body, n_col, 16),
        [shape((group, width), BF16), shape((rows, width), BF16)],
        1,
        n_col + 8,
        scratch=[
            pltpu.VMEM((region, width), F32),
            pltpu.VMEM((ATOM_HEADS * (group + 2 * HALO_BIAS * rows), KWIN), BF16),
            pltpu.VMEM((region, width), BF16),
            pltpu.VMEM((region, width), BF16),
            pltpu.VMEM((region, width), BF16),
            pltpu.VMEM((region, width), BF16),
            pltpu.VMEM((region, width), F32),
        ],
        name="atoms",
        vmem=24 << 20,
        flops=6 * region * width * width * 2 * 10,
        nbytes=4 * region * width * 2,
    )(col_at, *pieces, low, high, atom_norms, w_atom_qkv, w_atom_gate, w_atom_out, w_atom_up, w_atom_down)
    groups = gather(row_out, "row", ring)

    total = group * n_row
    size = min(total, 1024)
    channels = w_agg.shape[1]
    token_out = call(
        functools.partial(token_body, n_row, n_col, tile, heads),
        shape((tile, w_token.shape[2]), BF16),
        2,
        n_row + n_col + 4,
        scratch=[
            pltpu.VMEM((total, width), BF16),
            pltpu.VMEM((size, channels), BF16),
            pltpu.VMEM((n_tok, channels), F32),
            pltpu.VMEM((n_tok, 128), F32),
            pltpu.VMEM((n_tok, channels), BF16),
            pltpu.VMEM((n_tok, w_token.shape[2]), BF16),
            pltpu.VMEM((n_tok, w_token.shape[2]), BF16),
            pltpu.VMEM((n_tok, tile * heads), F32),
        ],
        name="tokens",
        vmem=40 << 20,
        flops=2 * total * width * channels,
        nbytes=2 * w_token.size,
    )(
        row_at,
        col_at,
        *groups,
        *tiles,
        atom_token.reshape(-1, size),
        w_agg,
        token_norm.reshape(1, -1),
        w_token,
    )
    return (atom_out, token_out)


def solution(mesh):
    placed = (
        P(("parts", "row", "col"), None),
        P(None, ("parts", "row", "col"), None),
        P(("parts", "row", "col"), None),
        P("parts"),
        P("parts"),
        P(("parts", "row"), "col", None),
    ) + (P(),) * 13
    return jax.shard_map(
        per_device,
        mesh=mesh,
        in_specs=placed,
        out_specs=(P(("parts", "row", "col"), None), P(("parts", "row"), None)),
        check_vma=False,
    )
```

```python
import functools

import jax
import jax.numpy as jnp
from jax import lax
from jax.experimental import pallas as pl
from jax.experimental.pallas import tpu as pltpu
from jax.sharding import PartitionSpec as P


ATOM_HEADS = 4
ATOM_BLOCKS = 3
QWIN = 32
KWIN = 128
TRANS = 2
MARGIN = (KWIN - QWIN) // 2
HALO_FEATS = 3
HALO_BIAS = 2

EPSILON = 1e-05
NEGATIVE = -1e30


VMEM = pl.BlockSpec(memory_space=pltpu.VMEM)
SMEM = pl.BlockSpec(memory_space=pltpu.SMEM)
HBM = pl.BlockSpec(memory_space=pltpu.HBM)
F32 = jnp.float32
BF16 = jnp.bfloat16


def nt(a, b):
    return lax.dot_general(a, b, (((1,), (1,)), ((), ())), preferred_element_type=F32)


def tn(a, b):
    return lax.dot_general(a, b, (((0,), (0,)), ((), ())), preferred_element_type=F32)


def mm(a, b):
    return jnp.dot(a, b, preferred_element_type=F32)


def norm_rows(x, gain):
    average = jnp.mean(x, axis=-1, keepdims=True)
    centered = x - average
    variance = jnp.mean(centered * centered, axis=-1, keepdims=True)
    return centered * lax.rsqrt(variance + EPSILON) * gain


def norm_wide(x, gain, ones):
    centered = x - jnp.mean(x, axis=-1, keepdims=True)
    squares = centered * centered
    high = squares.astype(BF16)
    low = (squares - high.astype(F32)).astype(BF16)
    variance = mm(jnp.concatenate([high, low], axis=1), ones)
    return centered * lax.rsqrt(variance + EPSILON) * gain


def sigmoid(x):
    return 0.5 * jnp.tanh(0.5 * x) + 0.5


def gated(first, second):
    half = 0.5 * first
    return ((half * jnp.tanh(half) + half) * second).astype(BF16)


def call(body, out_shape, n_smem, n_vmem, scratch=(), flops=0, nbytes=0, vmem=None):
    return pl.pallas_call(
        body,
        out_shape=out_shape,
        in_specs=[SMEM] * n_smem + [VMEM] * n_vmem,
        out_specs=jax.tree.map(lambda _: VMEM, out_shape),
        scratch_shapes=list(scratch),
        cost_estimate=pl.CostEstimate(flops=flops, bytes_accessed=nbytes, transcendentals=0),
        compiler_params=pltpu.CompilerParams(vmem_limit_bytes=vmem) if vmem else None,
    )


def pack_body(n_row, n_col, row, col, bias, mask, feats, out, bias_v, mask_v, sems):
    rows = feats.shape[0]
    copies = [
        pltpu.make_async_copy(source, target, sems.at[i])
        for i, (source, target) in enumerate(((mask, mask_v), (bias, bias_v), (feats, out.at[0:rows])))
    ]
    for copy in copies:
        copy.start()
    for copy in copies:
        copy.wait()
    total_atoms = n_row * n_col * rows
    begin = (row[0] * n_col + col[0]) * rows
    slot = lax.broadcasted_iota(jnp.int32, (1, KWIN), 1)
    own = (slot >= MARGIN) & (slot < MARGIN + QWIN)
    for w in range(rows // QWIN):
        index = begin + w * QWIN - MARGIN + slot
        usable = ((index >= 0) & (index < total_atoms) & (mask_v[w : w + 1, :] == 1)) | own
        keep = jnp.broadcast_to(usable, (QWIN, KWIN))
        for h in range(ATOM_HEADS):
            part = bias_v[h, w * QWIN : (w + 1) * QWIN, :].astype(F32)
            at = rows + (w * ATOM_HEADS + h) * QWIN
            out[at : at + QWIN, :] = jnp.where(keep, part, NEGATIVE).astype(BF16)


def ends_body(n_col, rows, row, col, *refs):
    pieces, (near, far) = refs[:n_col], refs[n_col:]
    feats, fat = HALO_FEATS * rows, ATOM_HEADS * rows
    even = lax.rem(row[0], 2) == 0
    for k in range(n_col):
        at = col[0] ^ k
        back = at - (n_col - HALO_FEATS)

        def left(out):
            @pl.when(at < HALO_FEATS)
            def _():
                out[pl.ds(pl.multiple_of(at * rows, rows), rows)] = pieces[k][0:rows]

            @pl.when(at < HALO_BIAS)
            def _():
                out[pl.ds(pl.multiple_of(feats + at * fat, rows), fat)] = pieces[k][rows:]

        def right(out):
            @pl.when(back >= 0)
            def _():
                out[pl.ds(pl.multiple_of(back * rows, rows), rows)] = pieces[k][0:rows]

            @pl.when(back >= HALO_FEATS - HALO_BIAS)
            def _():
                spot = feats + (back - (HALO_FEATS - HALO_BIAS)) * fat
                out[pl.ds(pl.multiple_of(spot, rows), fat)] = pieces[k][rows:]

        @pl.when(even)
        def _():
            right(near)
            left(far)

        @pl.when(jnp.logical_not(even))
        def _():
            left(near)
            right(far)


def atom_body(n_col, together, row, col, *refs):
    pieces = refs[:n_col]
    near, far, norms, w_qkv, w_gate, w_out, w_up, w_down, row_out, own_out = refs[n_col : n_col + 10]
    state, bias, normed_s, keys_s, vals_s, query_s, att_s = refs[n_col + 10 :]
    rows, width = own_out.shape
    group = row_out.shape[0]
    head = width // ATOM_HEADS
    ext = HALO_FEATS * rows
    bext = HALO_BIAS * rows
    fat = ATOM_HEADS * rows
    even = lax.rem(row[0], 2) == 0
    above = ext + group
    for half, at in ((near, jnp.where(even, above, 0)), (far, jnp.where(even, 0, above))):
        state[pl.ds(pl.multiple_of(at, rows), ext)] = half[0:ext].astype(F32)
        at = jnp.where(at == 0, 0, (bext + group) * ATOM_HEADS)
        bias[pl.ds(pl.multiple_of(at, rows), HALO_BIAS * fat)] = half[ext:]
    for k in range(n_col):
        at = (col[0] ^ k) * rows
        state[pl.ds(pl.multiple_of(ext + at, rows), rows)] = pieces[k][0:rows].astype(F32)
        bias[pl.ds(pl.multiple_of((bext + at) * ATOM_HEADS, rows), fat)] = pieces[k][rows:]
    ones = jnp.full((2 * width, width), 1.0 / width, BF16)
    lane = lax.broadcasted_iota(jnp.int32, (1, width), 1)
    scale = 1.0 / (head**0.5)
    tall = ATOM_HEADS * QWIN
    for block in range(ATOM_BLOCKS):
        rest = (ATOM_BLOCKS - 1 - block) * rows
        count = group + 2 * rest
        first = ext - rest
        base = first - MARGIN
        span = count + 2 * MARGIN
        bias_at = (bext - rest) * ATOM_HEADS
        normed = norm_wide(state[base : base + span], norms[block, 0:1], ones).astype(BF16)
        normed_s[0:span] = normed
        qkv = mm(normed, w_qkv[block])
        query_s[0:span] = qkv[:, :width].astype(BF16)
        keys_s[0:span] = qkv[:, width : 2 * width].astype(BF16)
        vals_s[0:span] = qkv[:, 2 * width :].astype(BF16)
        n_win = count // QWIN
        for start in range(0, n_win, together):
            spots = [w * QWIN for w in range(start, min(start + together, n_win))]
            parts = []
            for at in spots:
                query = query_s[at + MARGIN : at + MARGIN + QWIN]
                spread = jnp.concatenate(
                    [jnp.where(lane // head == h, query, jnp.zeros_like(query)) for h in range(ATOM_HEADS)],
                    axis=0,
                )
                parts.append(nt(spread, keys_s[at : at + KWIN]))
            bias_row = bias_at + start * tall
            extra = bias[bias_row : bias_row + len(spots) * tall].astype(F32)
            scores = jnp.concatenate(parts, axis=0) * scale + extra
            weights = jnp.exp(scores - jnp.max(scores, axis=-1, keepdims=True))
            totals = jnp.sum(weights, axis=-1, keepdims=True)
            weights = weights.astype(BF16)
            for i, at in enumerate(spots):
                mixed = mm(weights[i * tall : (i + 1) * tall], vals_s[at : at + KWIN])
                total = jnp.broadcast_to(totals[i * tall : (i + 1) * tall], (tall, width))
                weighted, divisor = mixed[:QWIN], total[:QWIN]
                for h in range(1, ATOM_HEADS):
                    mine = lane // head == h
                    weighted = jnp.where(mine, mixed[h * QWIN : (h + 1) * QWIN], weighted)
                    divisor = jnp.where(mine, total[h * QWIN : (h + 1) * QWIN], divisor)
                att_s[at : at + QWIN] = weighted / divisor
        gates = sigmoid(mm(normed_s[MARGIN : MARGIN + count], w_gate[block]))
        mixed = (gates * att_s[0:count]).astype(BF16)
        now = state[first : first + count] + mm(mixed, w_out[block])
        normed_two = norm_wide(now, norms[block, 1:2], ones).astype(BF16)
        both = mm(normed_two, w_up[block])
        half = both.shape[1] // 2
        hidden = gated(both[:, :half], both[:, half:])
        state[first : first + count] = now + mm(hidden, w_down[block])
    row_out[...] = state[ext : ext + group].astype(BF16)
    own = pl.multiple_of(ext + col[0] * rows, rows)
    own_out[...] = state[pl.ds(own, rows)].astype(BF16)


def pair_body(row, col, *refs):
    n_load = 6
    given, out, given_v, sems = refs[:n_load], refs[n_load], refs[n_load + 1 : -1], refs[-1]
    copies = [pltpu.make_async_copy(given[i], given_v[i], sems.at[i]) for i in range(n_load)]
    for copy in copies:
        copy.start()
    live, pair, norms, w_up, w_down, w_bias = given_v
    for copy in copies[:3]:
        copy.wait()
    tile_q, tile_k, width = pair.shape
    ones = jnp.full((2 * width, width), 1.0 / width, BF16)
    z = pair[...].astype(F32).reshape(tile_q * tile_k, width)
    normed = norm_wide(z, norms[0:1], ones).astype(BF16)
    for copy in copies[3:]:
        copy.wait()
    heads = w_bias.shape[0]
    group = 128 // heads
    half = w_up.shape[2] // 2
    tall = jnp.concatenate([w_bias[...]] * group, axis=0)
    high = tall.astype(BF16)
    low = (tall - high.astype(F32)).astype(BF16)
    spread = jnp.concatenate(
        [jnp.concatenate([high, high], axis=1), jnp.concatenate([low, low], axis=1)], axis=0
    )
    lane = lax.broadcasted_iota(jnp.int32, (1, 128), 1)
    n_tok = live.shape[1]
    key_at = col[0] * tile_k + lax.broadcasted_iota(jnp.int32, (tile_k, n_tok), 0)
    spots = lax.broadcasted_iota(jnp.int32, (tile_k, n_tok), 1)
    seen = jnp.where(key_at == spots, live[...], 0).astype(F32)
    alive = jnp.sum(seen, axis=-1, keepdims=True) == 1.0
    key_index = col[0] * tile_k + lax.broadcasted_iota(jnp.int32, (tile_k, 128), 0)
    lane_full = lax.broadcasted_iota(jnp.int32, (tile_k, 128), 1)
    for m in range(TRANS):
        if m > 0:
            normed = norm_wide(z, norms[m : m + 1], ones).astype(BF16)
        both = mm(normed, w_up[m])
        z = z + mm(gated(both[:, :half], both[:, half:]), w_down[m])
    final = norm_wide(z, norms[TRANS : TRANS + 1], ones)
    final_high = final.astype(BF16)
    final_low = (final - final_high.astype(F32)).astype(BF16)
    wide = nt(jnp.concatenate([final_high, final_low], axis=1), spread)
    summed = wide[:, :128] + wide[:, 128:]
    for g in range(tile_q // group):
        acc = jnp.zeros((tile_k, 128), F32)
        for i in range(group):
            at = (g * group + i) * tile_k
            acc = jnp.where(lane // heads == i, summed[at : at + tile_k], acc)
        query_index = row[0] * tile_q + g * group + lane_full // heads
        allowed = alive | (query_index == key_index)
        out[:, g * 128 : (g + 1) * 128] = jnp.where(allowed, acc, NEGATIVE)


def one_hot(n_tok, ids):
    token = lax.broadcasted_iota(jnp.int32, (n_tok, ids.shape[1]), 0)
    return jnp.where(token == ids, 1.0, 0.0)


def sums_body(n_row, row, own, ids, w_agg, sums, counts, *hots):
    n_tok = sums.shape[0]
    group = own.shape[0]
    number = jnp.zeros((n_tok, 1), F32)
    for k in range(n_row):
        source = lax.rem(row[0] + (n_row - k), n_row)
        hot = one_hot(n_tok, ids[pl.ds(source, 1), :])
        number = number + jnp.sum(hot, axis=-1, keepdims=True)
        hot = hot.astype(BF16)
        if k and hots:
            hots[0][:, (k - 1) * group : k * group] = hot
        elif not k:
            feat = jnp.maximum(mm(own[...], w_agg[...]), 0.0).astype(BF16)
            sums[...] = mm(hot, feat)
    counts[...] = jnp.broadcast_to(number, counts.shape)


def token_body(n_row, n_col, tile, heads, row, col, *refs):
    groups, tiles = refs[: n_row - 1], refs[n_row - 1 : n_row - 1 + n_col]
    sums, counts, hots, w_agg, gain, w_token, out = refs[n_row - 1 + n_col : n_row + n_col + 6]
    feat, tokens, keys, vals, bias = refs[n_row + n_col + 6 :]
    group = groups[0].shape[0]
    for k in range(n_col):
        at = (col[0] ^ k) * tile
        bias[pl.ds(pl.multiple_of(at, tile), tile)] = tiles[k][...]
    total = sums[...]
    many = feat.shape[0] // group
    for start in range(0, n_row - 1, many):
        some = groups[start : start + many]
        for i, part in enumerate(some):
            product = mm(part[...], w_agg[...])
            feat[i * group : (i + 1) * group] = jnp.maximum(product, 0.0).astype(BF16)
        size = len(some) * group
        if hots.shape[0] == total.shape[0]:
            hot = hots[:, start * group : start * group + size]
        else:
            source = lax.rem(row[0] + (n_row - 1 - start), n_row)
            hot = one_hot(total.shape[0], hots[pl.ds(source, 1), :]).astype(BF16)
        total = total + mm(hot, feat[0:size])
    tokens[...] = norm_rows(total * (1.0 / counts[:, 0:1]), gain[...]).astype(BF16)
    keys[...] = mm(tokens[...], w_token[1]).astype(BF16)
    vals[...] = mm(tokens[...], w_token[2]).astype(BF16)
    mine = tokens[pl.ds(pl.multiple_of(row[0] * tile, tile), tile)]
    query = mm(mine, w_token[0]).astype(BF16).astype(F32)
    gates = sigmoid(mm(mine, w_token[3]).astype(BF16).astype(F32))
    width = query.shape[1]
    head = width // heads
    lane = lax.broadcasted_iota(jnp.int32, (heads, width), 1)
    which = lax.broadcasted_iota(jnp.int32, (heads, width), 0)
    own = (lane >= which * head) & (lane < (which + 1) * head)
    own = jnp.broadcast_to(own[None], (tile, heads, width))
    spread = jnp.where(own, query[:, None, :], 0.0).reshape(tile * heads, width).astype(BF16)
    scores = nt(keys[...], spread) * (1.0 / head**0.5) + bias[...]
    top = jnp.max(scores, axis=0, keepdims=True)
    weights = jnp.exp(scores - top)
    total_w = jnp.sum(weights, axis=0, keepdims=True)
    mixed = tn(weights.astype(BF16), vals[...])
    inverse = jnp.transpose(jnp.broadcast_to(1.0 / total_w, (8, tile * heads)))[:, 0:1]
    mixed = (mixed * inverse).reshape(tile, heads, width)
    attended = jnp.sum(jnp.where(own, mixed, 0.0), axis=1)
    out[...] = (gates * attended).astype(BF16)


def in_hbm(value):
    return pltpu.with_memory_space_constraint(value, pltpu.HBM)


def permute(value, axis, target):
    pairs = [(i, target(i)) for i in range(lax.axis_size(axis))]
    return lax.ppermute(value, axis, pairs)


def gather(value, axis, partner):
    count = lax.axis_size(axis)
    return [value] + [
        permute(value, axis, functools.partial(partner, k, count)) for k in range(1, count)
    ]


def ring(k, count, i):
    return (i + k) % count


def swap(k, count, i):
    return i ^ k


def beyond(count, i):
    other = i + 1 if i % 2 else i - 1
    return other if 0 <= other < count else i


def per_device(
    atom_feats,
    atom_bias,
    key_mask,
    atom_token,
    token_mask,
    pair,
    atom_norms,
    w_atom_qkv,
    w_atom_gate,
    w_atom_out,
    w_atom_up,
    w_atom_down,
    w_agg,
    token_norm,
    w_token,
    pair_norms,
    w_pair_up,
    w_pair_down,
    w_bias,
):
    rows, width = atom_feats.shape
    n_row, n_col = lax.axis_size("row"), lax.axis_size("col")
    row, col = lax.axis_index("row").astype(jnp.int32), lax.axis_index("col").astype(jnp.int32)
    n_tok = token_mask.shape[0]
    tile = pair.shape[0]
    heads = w_bias.shape[1]
    planes = 1 + ATOM_HEADS
    group = rows * n_col
    shape = jax.ShapeDtypeStruct

    row_at, col_at = row.reshape(1), col.reshape(1)
    assert n_col & (n_col - 1) == 0 and n_col >= HALO_FEATS
    for_pair = (token_mask.reshape(1, -1), pair, pair_norms, w_pair_up, w_pair_down, w_bias.T)
    packed = pl.pallas_call(
        functools.partial(pack_body, n_row, n_col),
        out_shape=shape((planes * rows, width), BF16),
        in_specs=[SMEM] * 2 + [HBM] * 3,
        out_specs=VMEM,
        scratch_shapes=[
            pltpu.VMEM(atom_bias.shape, BF16),
            pltpu.VMEM(key_mask.shape, jnp.int32),
            pltpu.SemaphoreType.DMA((3,)),
        ],
        compiler_params=pltpu.CompilerParams(vmem_limit_bytes=4 << 20),
        name="pack",
    )(row_at, col_at, *map(in_hbm, (atom_bias, key_mask, atom_feats)))
    pieces = gather(packed, "col", swap)

    packed, *for_pair = lax.optimization_barrier((packed, *for_pair))
    pair_out = pl.pallas_call(
        pair_body,
        out_shape=shape((pair.shape[1], tile * heads), F32),
        in_specs=[SMEM] * 2 + [HBM] * len(for_pair),
        out_specs=VMEM,
        scratch_shapes=[pltpu.VMEM(x.shape, x.dtype) for x in for_pair]
        + [pltpu.SemaphoreType.DMA((len(for_pair),))],
        cost_estimate=pl.CostEstimate(
            flops=2 * pair.size * w_pair_up.shape[2] * 3, bytes_accessed=0, transcendentals=0
        ),
        compiler_params=pltpu.CompilerParams(vmem_limit_bytes=32 << 20),
        name="pair",
    )(row_at, col_at, *map(in_hbm, for_pair))
    *pieces, pair_out = lax.optimization_barrier((*pieces, pair_out))
    halo = (HALO_FEATS + ATOM_HEADS * HALO_BIAS) * rows
    near, far = call(
        functools.partial(ends_body, n_col, rows),
        [shape((halo, width), BF16)] * 2,
        2,
        n_col,
        vmem=8 << 20,
    )(row_at, col_at, *pieces)
    near_in = permute(near, "row", lambda i: i ^ 1)
    far_in = permute(far, "row", lambda i: beyond(n_row, i))
    tiles = gather(pair_out, "col", swap)

    region = group + 2 * HALO_FEATS * rows
    row_out, atom_out = call(
        functools.partial(atom_body, n_col, 16),
        [shape((group, width), BF16), shape((rows, width), BF16)],
        2,
        n_col + 8,
        scratch=[
            pltpu.VMEM((region, width), F32),
            pltpu.VMEM((ATOM_HEADS * (group + 2 * HALO_BIAS * rows), KWIN), BF16),
            pltpu.VMEM((region, width), BF16),
            pltpu.VMEM((region, width), BF16),
            pltpu.VMEM((region, width), BF16),
            pltpu.VMEM((region, width), BF16),
            pltpu.VMEM((region, width), F32),
        ],
        vmem=24 << 20,
        flops=6 * region * width * width * 2 * 10,
        nbytes=4 * region * width * 2,
    )(row_at, col_at, *pieces, near_in, far_in, atom_norms, w_atom_qkv, w_atom_gate, w_atom_out, w_atom_up, w_atom_down)
    groups = gather(row_out, "row", ring)

    channels, joined = w_agg.shape[1], w_token.shape[2]
    ids = atom_token.reshape(n_row, group)
    outs = [shape((n_tok, channels), F32), shape((n_tok, 128), F32)]
    few = n_row <= 4
    if few:
        outs.append(shape((n_tok, (n_row - 1) * group), BF16))
    sums, counts, *hots = call(
        functools.partial(sums_body, n_row),
        outs,
        1,
        3,
        vmem=8 << 20,
        flops=2 * group * n_tok * channels,
    )(row_at, row_out, ids, w_agg)
    token_out = call(
        functools.partial(token_body, n_row, n_col, tile, heads),
        shape((tile, joined), BF16),
        2,
        n_row + n_col + 5,
        scratch=[
            pltpu.VMEM(((n_row - 1 if few else 1) * group, channels), BF16),
            pltpu.VMEM((n_tok, channels), BF16),
            pltpu.VMEM((n_tok, joined), BF16),
            pltpu.VMEM((n_tok, joined), BF16),
            pltpu.VMEM((n_tok, tile * heads), F32),
        ],
        flops=2 * (n_row - 1) * group * width * channels,
        vmem=24 << 20,
    )(
        row_at,
        col_at,
        *groups[1:],
        *tiles,
        sums,
        counts,
        *(hots or [ids]),
        w_agg,
        token_norm.reshape(1, -1),
        w_token,
    )
    return (atom_out, token_out)


def solution(mesh):
    placed = (
        P(("parts", "row", "col"), None),
        P(None, ("parts", "row", "col"), None),
        P(("parts", "row", "col"), None),
        P("parts"),
        P("parts"),
        P(("parts", "row"), "col", None),
    ) + (P(),) * 13
    return jax.shard_map(
        per_device,
        mesh=mesh,
        in_specs=placed,
        out_specs=(P(("parts", "row", "col"), None), P(("parts", "row"), None)),
        check_vma=False,
    )
```

```python
import functools

import jax
import jax.numpy as jnp
from jax import lax
from jax.experimental import pallas as pl
from jax.experimental.pallas import tpu as pltpu
from jax.sharding import PartitionSpec as P


ATOM_HEADS = 4
ATOM_BLOCKS = 3
QWIN = 32
KWIN = 128
TRANS = 2
MARGIN = (KWIN - QWIN) // 2
HALO_FEATS = 3
HALO_BIAS = 2

EPSILON = 1e-05
NEGATIVE = -1e30


VMEM = pl.BlockSpec(memory_space=pltpu.VMEM)
SMEM = pl.BlockSpec(memory_space=pltpu.SMEM)
HBM = pl.BlockSpec(memory_space=pltpu.HBM)
F32 = jnp.float32
BF16 = jnp.bfloat16


def nt(a, b):
    return lax.dot_general(a, b, (((1,), (1,)), ((), ())), preferred_element_type=F32)


def tn(a, b):
    return lax.dot_general(a, b, (((0,), (0,)), ((), ())), preferred_element_type=F32)


def mm(a, b):
    return jnp.dot(a, b, preferred_element_type=F32)


def norm_rows(x, gain):
    average = jnp.mean(x, axis=-1, keepdims=True)
    centered = x - average
    variance = jnp.mean(centered * centered, axis=-1, keepdims=True)
    return centered * lax.rsqrt(variance + EPSILON) * gain


def norm_wide(x, gain, ones):
    centered = x - jnp.mean(x, axis=-1, keepdims=True)
    squares = centered * centered
    high = squares.astype(BF16)
    low = (squares - high.astype(F32)).astype(BF16)
    variance = mm(jnp.concatenate([high, low], axis=1), ones)
    return centered * lax.rsqrt(variance + EPSILON) * gain


def sigmoid(x):
    return 0.5 * jnp.tanh(0.5 * x) + 0.5


def gated(first, second):
    half = 0.5 * first
    return ((half * jnp.tanh(half) + half) * second).astype(BF16)


def call(body, out_shape, n_smem, n_vmem, scratch=(), flops=0, nbytes=0, vmem=None):
    return pl.pallas_call(
        body,
        out_shape=out_shape,
        in_specs=[SMEM] * n_smem + [VMEM] * n_vmem,
        out_specs=jax.tree.map(lambda _: VMEM, out_shape),
        scratch_shapes=list(scratch),
        cost_estimate=pl.CostEstimate(flops=flops, bytes_accessed=nbytes, transcendentals=0),
        compiler_params=pltpu.CompilerParams(vmem_limit_bytes=vmem) if vmem else None,
    )


def pack_body(n_row, n_col, n_load, row, col, bias, mask, feats, *refs):
    loads, out, loaded = refs[:n_load], refs[n_load], refs[n_load + 1 : 2 * n_load + 1]
    bias_v, mask_v, sems = refs[2 * n_load + 1 :]
    rows = feats.shape[0]
    moves = ((mask, mask_v), (bias, bias_v), (feats, out.at[0:rows]), *zip(loads, loaded))
    copies = [pltpu.make_async_copy(a, b, sems.at[i]) for i, (a, b) in enumerate(moves)]
    for copy in copies:
        copy.start()
    for copy in copies[:3]:
        copy.wait()
    total_atoms = n_row * n_col * rows
    begin = (row[0] * n_col + col[0]) * rows
    slot = lax.broadcasted_iota(jnp.int32, (1, KWIN), 1)
    own = (slot >= MARGIN) & (slot < MARGIN + QWIN)
    for w in range(rows // QWIN):
        index = begin + w * QWIN - MARGIN + slot
        usable = ((index >= 0) & (index < total_atoms) & (mask_v[w : w + 1, :] == 1)) | own
        keep = jnp.broadcast_to(usable, (QWIN, KWIN))
        for h in range(ATOM_HEADS):
            part = bias_v[h, w * QWIN : (w + 1) * QWIN, :].astype(F32)
            at = rows + (w * ATOM_HEADS + h) * QWIN
            out[at : at + QWIN, :] = jnp.where(keep, part, NEGATIVE).astype(BF16)
    for copy in copies[3:]:
        copy.wait()


def ends_body(n_col, rows, row, col, *refs):
    pieces, (near, far) = refs[:n_col], refs[n_col:]
    feats, fat = HALO_FEATS * rows, ATOM_HEADS * rows
    even = lax.rem(row[0], 2) == 0
    for k in range(n_col):
        at = col[0] ^ k
        back = at - (n_col - HALO_FEATS)

        def left(out):
            @pl.when(at < HALO_FEATS)
            def _():
                out[pl.ds(pl.multiple_of(at * rows, rows), rows)] = pieces[k][0:rows]

            @pl.when(at < HALO_BIAS)
            def _():
                out[pl.ds(pl.multiple_of(feats + at * fat, rows), fat)] = pieces[k][rows:]

        def right(out):
            @pl.when(back >= 0)
            def _():
                out[pl.ds(pl.multiple_of(back * rows, rows), rows)] = pieces[k][0:rows]

            @pl.when(back >= HALO_FEATS - HALO_BIAS)
            def _():
                spot = feats + (back - (HALO_FEATS - HALO_BIAS)) * fat
                out[pl.ds(pl.multiple_of(spot, rows), fat)] = pieces[k][rows:]

        @pl.when(even)
        def _():
            right(near)
            left(far)

        @pl.when(jnp.logical_not(even))
        def _():
            left(near)
            right(far)


def atom_body(n_col, together, row, col, *refs):
    pieces = refs[:n_col]
    near, far, norms, w_qkv, w_gate, w_out, w_up, w_down, row_out, own_out = refs[n_col : n_col + 10]
    state, bias, normed_s, keys_s, vals_s, query_s, att_s = refs[n_col + 10 :]
    rows, width = own_out.shape
    group = row_out.shape[0]
    head = width // ATOM_HEADS
    ext = HALO_FEATS * rows
    bext = HALO_BIAS * rows
    fat = ATOM_HEADS * rows
    even = lax.rem(row[0], 2) == 0
    above = ext + group
    for half, at in ((near, jnp.where(even, above, 0)), (far, jnp.where(even, 0, above))):
        state[pl.ds(pl.multiple_of(at, rows), ext)] = half[0:ext].astype(F32)
        at = jnp.where(at == 0, 0, (bext + group) * ATOM_HEADS)
        bias[pl.ds(pl.multiple_of(at, rows), HALO_BIAS * fat)] = half[ext:]
    for k in range(n_col):
        at = (col[0] ^ k) * rows
        state[pl.ds(pl.multiple_of(ext + at, rows), rows)] = pieces[k][0:rows].astype(F32)
        bias[pl.ds(pl.multiple_of((bext + at) * ATOM_HEADS, rows), fat)] = pieces[k][rows:]
    ones = jnp.full((2 * width, width), 1.0 / width, BF16)
    lane = lax.broadcasted_iota(jnp.int32, (1, width), 1)
    scale = 1.0 / (head**0.5)
    tall = ATOM_HEADS * QWIN
    for block in range(ATOM_BLOCKS):
        rest = (ATOM_BLOCKS - 1 - block) * rows
        count = group + 2 * rest
        first = ext - rest
        base = first - MARGIN
        span = count + 2 * MARGIN
        bias_at = (bext - rest) * ATOM_HEADS
        normed = norm_wide(state[base : base + span], norms[block, 0:1], ones).astype(BF16)
        normed_s[0:span] = normed
        qkv = mm(normed, w_qkv[block])
        query_s[0:span] = qkv[:, :width].astype(BF16)
        keys_s[0:span] = qkv[:, width : 2 * width].astype(BF16)
        vals_s[0:span] = qkv[:, 2 * width :].astype(BF16)
        n_win = count // QWIN
        for start in range(0, n_win, together):
            spots = [w * QWIN for w in range(start, min(start + together, n_win))]
            parts = []
            for at in spots:
                query = query_s[at + MARGIN : at + MARGIN + QWIN]
                spread = jnp.concatenate(
                    [jnp.where(lane // head == h, query, jnp.zeros_like(query)) for h in range(ATOM_HEADS)],
                    axis=0,
                )
                parts.append(nt(spread, keys_s[at : at + KWIN]))
            bias_row = bias_at + start * tall
            extra = bias[bias_row : bias_row + len(spots) * tall].astype(F32)
            scores = jnp.concatenate(parts, axis=0) * scale + extra
            weights = jnp.exp(scores - jnp.max(scores, axis=-1, keepdims=True))
            totals = jnp.sum(weights, axis=-1, keepdims=True)
            weights = weights.astype(BF16)
            for i, at in enumerate(spots):
                mixed = mm(weights[i * tall : (i + 1) * tall], vals_s[at : at + KWIN])
                total = jnp.broadcast_to(totals[i * tall : (i + 1) * tall], (tall, width))
                weighted, divisor = mixed[:QWIN], total[:QWIN]
                for h in range(1, ATOM_HEADS):
                    mine = lane // head == h
                    weighted = jnp.where(mine, mixed[h * QWIN : (h + 1) * QWIN], weighted)
                    divisor = jnp.where(mine, total[h * QWIN : (h + 1) * QWIN], divisor)
                att_s[at : at + QWIN] = weighted / divisor
        gates = sigmoid(mm(normed_s[MARGIN : MARGIN + count], w_gate[block]))
        mixed = (gates * att_s[0:count]).astype(BF16)
        now = state[first : first + count] + mm(mixed, w_out[block])
        normed_two = norm_wide(now, norms[block, 1:2], ones).astype(BF16)
        both = mm(normed_two, w_up[block])
        half = both.shape[1] // 2
        hidden = gated(both[:, :half], both[:, half:])
        state[first : first + count] = now + mm(hidden, w_down[block])
    row_out[...] = state[ext : ext + group].astype(BF16)
    own = pl.multiple_of(ext + col[0] * rows, rows)
    own_out[...] = state[pl.ds(own, rows)].astype(BF16)


def pair_body(n_early, row, col, *refs):
    early, rest = refs[:n_early], refs[n_early:]
    n_late = 6 - n_early
    late, out, late_v = rest[:n_late], rest[n_late], rest[n_late + 1 : 2 * n_late + 1]
    copies = [pltpu.make_async_copy(late[i], late_v[i], rest[-1].at[i]) for i in range(n_late)]
    for copy in copies:
        copy.start()
    live, pair, norms, w_up, w_down, w_bias = (*early, *late_v)
    tile_q, tile_k, width = pair.shape
    ones = jnp.full((2 * width, width), 1.0 / width, BF16)
    z = pair[...].astype(F32).reshape(tile_q * tile_k, width)
    normed = norm_wide(z, norms[0:1], ones).astype(BF16)
    for copy in copies:
        copy.wait()
    heads = w_bias.shape[0]
    group = 128 // heads
    half = w_up.shape[2] // 2
    tall = jnp.concatenate([w_bias[...]] * group, axis=0)
    high = tall.astype(BF16)
    low = (tall - high.astype(F32)).astype(BF16)
    spread = jnp.concatenate(
        [jnp.concatenate([high, high], axis=1), jnp.concatenate([low, low], axis=1)], axis=0
    )
    lane = lax.broadcasted_iota(jnp.int32, (1, 128), 1)
    n_tok = live.shape[1]
    key_at = col[0] * tile_k + lax.broadcasted_iota(jnp.int32, (tile_k, n_tok), 0)
    spots = lax.broadcasted_iota(jnp.int32, (tile_k, n_tok), 1)
    seen = jnp.where(key_at == spots, live[...], 0).astype(F32)
    alive = jnp.sum(seen, axis=-1, keepdims=True) == 1.0
    key_index = col[0] * tile_k + lax.broadcasted_iota(jnp.int32, (tile_k, 128), 0)
    lane_full = lax.broadcasted_iota(jnp.int32, (tile_k, 128), 1)
    for m in range(TRANS):
        if m > 0:
            normed = norm_wide(z, norms[m : m + 1], ones).astype(BF16)
        both = mm(normed, w_up[m])
        z = z + mm(gated(both[:, :half], both[:, half:]), w_down[m])
    final = norm_wide(z, norms[TRANS : TRANS + 1], ones)
    final_high = final.astype(BF16)
    final_low = (final - final_high.astype(F32)).astype(BF16)
    wide = nt(jnp.concatenate([final_high, final_low], axis=1), spread)
    summed = wide[:, :128] + wide[:, 128:]
    for g in range(tile_q // group):
        acc = jnp.zeros((tile_k, 128), F32)
        for i in range(group):
            at = (g * group + i) * tile_k
            acc = jnp.where(lane // heads == i, summed[at : at + tile_k], acc)
        query_index = row[0] * tile_q + g * group + lane_full // heads
        allowed = alive | (query_index == key_index)
        out[:, g * 128 : (g + 1) * 128] = jnp.where(allowed, acc, NEGATIVE)


def one_hot(n_tok, ids):
    token = lax.broadcasted_iota(jnp.int32, (n_tok, ids.shape[1]), 0)
    return jnp.where(token == ids, 1.0, 0.0)


def sums_body(n_row, row, own, ids, w_agg, sums, counts, *hots):
    n_tok = sums.shape[0]
    group = own.shape[0]
    number = jnp.zeros((n_tok, 1), F32)
    for k in range(n_row):
        source = lax.rem(row[0] + (n_row - k), n_row)
        hot = one_hot(n_tok, ids[pl.ds(source, 1), :])
        number = number + jnp.sum(hot, axis=-1, keepdims=True)
        hot = hot.astype(BF16)
        if k and hots:
            hots[0][:, (k - 1) * group : k * group] = hot
        elif not k:
            feat = jnp.maximum(mm(own[...], w_agg[...]), 0.0).astype(BF16)
            sums[...] = mm(hot, feat)
    counts[...] = jnp.broadcast_to(number, counts.shape)


def token_body(n_row, n_col, tile, heads, row, col, *refs):
    groups, tiles = refs[: n_row - 1], refs[n_row - 1 : n_row - 1 + n_col]
    sums, counts, hots, w_agg, gain, w_token, out = refs[n_row - 1 + n_col : n_row + n_col + 6]
    feat, tokens, keys, vals, bias = refs[n_row + n_col + 6 :]
    group = groups[0].shape[0]
    for k in range(n_col):
        at = (col[0] ^ k) * tile
        bias[pl.ds(pl.multiple_of(at, tile), tile)] = tiles[k][...]
    total = sums[...]
    many = feat.shape[0] // group
    for start in range(0, n_row - 1, many):
        some = groups[start : start + many]
        for i, part in enumerate(some):
            product = mm(part[...], w_agg[...])
            feat[i * group : (i + 1) * group] = jnp.maximum(product, 0.0).astype(BF16)
        size = len(some) * group
        if hots.shape[0] == total.shape[0]:
            hot = hots[:, start * group : start * group + size]
        else:
            source = lax.rem(row[0] + (n_row - 1 - start), n_row)
            hot = one_hot(total.shape[0], hots[pl.ds(source, 1), :]).astype(BF16)
        total = total + mm(hot, feat[0:size])
    tokens[...] = norm_rows(total * (1.0 / counts[:, 0:1]), gain[...]).astype(BF16)
    keys[...] = mm(tokens[...], w_token[1]).astype(BF16)
    vals[...] = mm(tokens[...], w_token[2]).astype(BF16)
    mine = tokens[pl.ds(pl.multiple_of(row[0] * tile, tile), tile)]
    query = mm(mine, w_token[0]).astype(BF16).astype(F32)
    gates = sigmoid(mm(mine, w_token[3]).astype(BF16).astype(F32))
    width = query.shape[1]
    head = width // heads
    lane = lax.broadcasted_iota(jnp.int32, (heads, width), 1)
    which = lax.broadcasted_iota(jnp.int32, (heads, width), 0)
    own = (lane >= which * head) & (lane < (which + 1) * head)
    own = jnp.broadcast_to(own[None], (tile, heads, width))
    spread = jnp.where(own, query[:, None, :], 0.0).reshape(tile * heads, width).astype(BF16)
    scores = nt(keys[...], spread) * (1.0 / head**0.5) + bias[...]
    top = jnp.max(scores, axis=0, keepdims=True)
    weights = jnp.exp(scores - top)
    total_w = jnp.sum(weights, axis=0, keepdims=True)
    mixed = tn(weights.astype(BF16), vals[...])
    inverse = jnp.transpose(jnp.broadcast_to(1.0 / total_w, (8, tile * heads)))[:, 0:1]
    mixed = (mixed * inverse).reshape(tile, heads, width)
    attended = jnp.sum(jnp.where(own, mixed, 0.0), axis=1)
    out[...] = (gates * attended).astype(BF16)


def in_hbm(value):
    return pltpu.with_memory_space_constraint(value, pltpu.HBM)


def permute(value, axis, target):
    pairs = [(i, target(i)) for i in range(lax.axis_size(axis))]
    return lax.ppermute(value, axis, pairs)


def gather(value, axis, partner):
    count = lax.axis_size(axis)
    return [value] + [
        permute(value, axis, functools.partial(partner, k, count)) for k in range(1, count)
    ]


def ring(k, count, i):
    return (i + k) % count


def swap(k, count, i):
    return i ^ k


def beyond(count, i):
    other = i + 1 if i % 2 else i - 1
    return other if 0 <= other < count else i


def per_device(
    atom_feats,
    atom_bias,
    key_mask,
    atom_token,
    token_mask,
    pair,
    atom_norms,
    w_atom_qkv,
    w_atom_gate,
    w_atom_out,
    w_atom_up,
    w_atom_down,
    w_agg,
    token_norm,
    w_token,
    pair_norms,
    w_pair_up,
    w_pair_down,
    w_bias,
):
    rows, width = atom_feats.shape
    n_row, n_col = lax.axis_size("row"), lax.axis_size("col")
    row, col = lax.axis_index("row").astype(jnp.int32), lax.axis_index("col").astype(jnp.int32)
    n_tok = token_mask.shape[0]
    tile = pair.shape[0]
    heads = w_bias.shape[1]
    planes = 1 + ATOM_HEADS
    group = rows * n_col
    shape = jax.ShapeDtypeStruct

    row_at, col_at = row.reshape(1), col.reshape(1)
    assert n_col & (n_col - 1) == 0 and n_col >= HALO_FEATS
    n_early = 6
    for_pair = (token_mask.reshape(1, -1), pair, pair_norms, w_pair_up, w_pair_down, w_bias.T)
    early, late = for_pair[:n_early], for_pair[n_early:]
    packed, *early = pl.pallas_call(
        functools.partial(pack_body, n_row, n_col, n_early),
        out_shape=[shape((planes * rows, width), BF16)] + [shape(x.shape, x.dtype) for x in early],
        in_specs=[SMEM] * 2 + [HBM] * (3 + n_early),
        out_specs=[VMEM] * (1 + n_early),
        scratch_shapes=[
            pltpu.VMEM(atom_bias.shape, BF16),
            pltpu.VMEM(key_mask.shape, jnp.int32),
            pltpu.SemaphoreType.DMA((3 + n_early,)),
        ],
        compiler_params=pltpu.CompilerParams(vmem_limit_bytes=4 << 20),
        name="pack",
    )(row_at, col_at, *map(in_hbm, (atom_bias, key_mask, atom_feats, *early)))
    pieces = gather(packed, "col", swap)

    packed, *late = lax.optimization_barrier((packed, *late))
    pair_out = pl.pallas_call(
        functools.partial(pair_body, n_early),
        out_shape=shape((pair.shape[1], tile * heads), F32),
        in_specs=[SMEM] * 2 + [VMEM] * n_early + [HBM] * len(late),
        out_specs=VMEM,
        scratch_shapes=[pltpu.VMEM(x.shape, x.dtype) for x in late]
        + ([pltpu.SemaphoreType.DMA((len(late),))] if late else []),
        cost_estimate=pl.CostEstimate(
            flops=2 * pair.size * w_pair_up.shape[2] * 3, bytes_accessed=0, transcendentals=0
        ),
        compiler_params=pltpu.CompilerParams(vmem_limit_bytes=32 << 20),
        name="pair",
    )(row_at, col_at, *early, *map(in_hbm, late))
    *pieces, pair_out = lax.optimization_barrier((*pieces, pair_out))
    halo = (HALO_FEATS + ATOM_HEADS * HALO_BIAS) * rows
    near, far = call(
        functools.partial(ends_body, n_col, rows),
        [shape((halo, width), BF16)] * 2,
        2,
        n_col,
        vmem=8 << 20,
    )(row_at, col_at, *pieces)
    near_in = permute(near, "row", lambda i: i ^ 1)
    far_in = permute(far, "row", lambda i: beyond(n_row, i))
    tiles = gather(pair_out, "col", swap)

    region = group + 2 * HALO_FEATS * rows
    row_out, atom_out = call(
        functools.partial(atom_body, n_col, 16),
        [shape((group, width), BF16), shape((rows, width), BF16)],
        2,
        n_col + 8,
        scratch=[
            pltpu.VMEM((region, width), F32),
            pltpu.VMEM((ATOM_HEADS * (group + 2 * HALO_BIAS * rows), KWIN), BF16),
            pltpu.VMEM((region, width), BF16),
            pltpu.VMEM((region, width), BF16),
            pltpu.VMEM((region, width), BF16),
            pltpu.VMEM((region, width), BF16),
            pltpu.VMEM((region, width), F32),
        ],
        vmem=24 << 20,
        flops=6 * region * width * width * 2 * 10,
        nbytes=4 * region * width * 2,
    )(row_at, col_at, *pieces, near_in, far_in, atom_norms, w_atom_qkv, w_atom_gate, w_atom_out, w_atom_up, w_atom_down)
    groups = gather(row_out, "row", ring)

    channels, joined = w_agg.shape[1], w_token.shape[2]
    ids = atom_token.reshape(n_row, group)
    outs = [shape((n_tok, channels), F32), shape((n_tok, 128), F32)]
    few = n_row <= 4
    if few:
        outs.append(shape((n_tok, (n_row - 1) * group), BF16))
    sums, counts, *hots = call(
        functools.partial(sums_body, n_row),
        outs,
        1,
        3,
        vmem=8 << 20,
        flops=2 * group * n_tok * channels,
    )(row_at, row_out, ids, w_agg)
    token_out = call(
        functools.partial(token_body, n_row, n_col, tile, heads),
        shape((tile, joined), BF16),
        2,
        n_row + n_col + 5,
        scratch=[
            pltpu.VMEM(((n_row - 1 if few else 1) * group, channels), BF16),
            pltpu.VMEM((n_tok, channels), BF16),
            pltpu.VMEM((n_tok, joined), BF16),
            pltpu.VMEM((n_tok, joined), BF16),
            pltpu.VMEM((n_tok, tile * heads), F32),
        ],
        flops=2 * (n_row - 1) * group * width * channels,
        vmem=24 << 20,
    )(
        row_at,
        col_at,
        *groups[1:],
        *tiles,
        sums,
        counts,
        *(hots or [ids]),
        w_agg,
        token_norm.reshape(1, -1),
        w_token,
    )
    return (atom_out, token_out)


def solution(mesh):
    placed = (
        P(("parts", "row", "col"), None),
        P(None, ("parts", "row", "col"), None),
        P(("parts", "row", "col"), None),
        P("parts"),
        P("parts"),
        P(("parts", "row"), "col", None),
    ) + (P(),) * 13
    return jax.shard_map(
        per_device,
        mesh=mesh,
        in_specs=placed,
        out_specs=(P(("parts", "row", "col"), None), P(("parts", "row"), None)),
        check_vma=False,
    )
```
